128 devices in a mesh: row: 8 (over y, core), feat: 16 (over x, z).
Axes of the slice: x: 4, y: 4, z: 4, core: 2. Of those that a mesh axis runs over, the one named last changes fastest.
Arguments:
- table_entries: bfloat16 [8192, 256, 128], P('row', 'feat'), may hold values from -6 to 6
- pseudo_points: bfloat16 [2, 128, 128], replicated, may hold values from -6 to 6
- projection_tensors: bfloat16 [2, 2, 4, 128, 128], replicated, may hold values from -0.5 to 0.5
- expanding_linear: bfloat16 [2, 2, 128, 256], replicated, may hold values from -0.5 to 0.5
- contracting_linear: bfloat16 [2, 2, 256, 128], replicated, may hold values from -0.375 to 0.375
- normalizer_multipliers: float32 [2, 4, 128], replicated, may hold values from 0.1 to 1.9
- sharpness_coefficients: float32 [2, 2, 4], replicated, may hold values from 2 to 12
Outputs:
- embedded: bfloat16 [8192, 256, 128], P(('row', 'feat'))
The draws below stay inside these ranges and needn't reach their ends.
All inputs are finite; a program needn't handle non-finite values.
Results may differ from the reference program's by a relative error of at most 0.02.
Values may be sent and summed in bfloat16 or wider, within the bound.
No kernel may reach another device: no remote copies, remote signals or barrier semaphores. Data moves between devices by JAX's collectives and lax.ppermute only.
A program may use at most 64 MiB of HBM per device.

```python
import math
import jax
import jax.numpy as jnp
from jax import lax

E = 128
M = 128
FOCUS_CHANNELS = 4
FF = 256
INDUCER_STACKS = 2
COLS = 256
ROWS = 8192


def shard_levels(rng, extent, cuts, low, largest):
    level = 1.0
    for axis_at, shards_of in cuts:
        steps = jax.random.uniform(jax.random.fold_in(jax.random.fold_in(rng, 6), axis_at), (shards_of,), jnp.float32, low / len(cuts), largest / len(cuts))
        level = level * jnp.repeat(jnp.exp(steps), extent[axis_at] // shards_of).reshape((-1,) + (1,) * (len(extent) - 1 - axis_at))
    return level


def noise(key, dims, scale, limit, cuts=(), held_as=jnp.bfloat16):
    gain = shard_levels(key, dims, cuts, -0.22, 0.18) if cuts else 1.0
    entries = jax.random.normal(key, dims, jnp.float32) * scale * gain
    return jnp.minimum(jnp.maximum(entries, -limit), limit).astype(held_as)


def setup_inputs(seed: int = 0) -> dict:
    seeds = jax.random.split(jax.random.key(seed), 8)
    return {
        "table_entries": noise(seeds[0], (ROWS, COLS, E), 1.0, 6.0, ((0, 8), (1, 16))),
        "pseudo_points": noise(seeds[1], (INDUCER_STACKS, M, E), 1.0, 6.0),
        "projection_tensors": noise(seeds[2], (INDUCER_STACKS, 2, 4, E, E), E ** -0.5, 0.5),
        "expanding_linear": noise(seeds[3], (INDUCER_STACKS, 2, E, FF), E ** -0.5, 0.5),
        "contracting_linear": noise(seeds[4], (INDUCER_STACKS, 2, FF, E), FF ** -0.5, 0.375),
        "normalizer_multipliers": jnp.clip(1.0 + 0.18 * jax.random.normal(seeds[5], (INDUCER_STACKS, 4, E), jnp.float32), 0.1, 1.9),
        "sharpness_coefficients": jnp.clip(jnp.exp(jax.random.uniform(seeds[6], (INDUCER_STACKS, 2, FOCUS_CHANNELS), jnp.float32, math.log(2.0), math.log(12.0))), 2.0, 12.0),
    }


def cast_to_half(values):
    return lax.optimization_barrier(values.astype(jnp.bfloat16))

def layer_norm(values, gain_row):
    values = values.astype(jnp.float32)
    center = values - lax.optimization_barrier(jnp.mean(values, axis=-1, keepdims=True))
    spread = lax.optimization_barrier(jnp.mean(center * center, axis=-1, keepdims=True))
    return center * lax.rsqrt(spread + 1e-05) * gain_row

def unit_rms(values):
    return values * lax.rsqrt(lax.optimization_barrier(jnp.mean(values * values, axis=-1, keepdims=True)) + 1e-06)

def partition_channels(values, channel_total):
    return values.reshape(values.shape[0], channel_total, values.shape[1] // channel_total)

def inducing_partials(normed, probe_vectors, key_weight, value_weight, multiplier_list):
    channel_total = multiplier_list.shape[0]
    head_width = probe_vectors.shape[1] // channel_total
    lookup_vectors = cast_to_half(unit_rms(jnp.dot(normed, key_weight, preferred_element_type=jnp.float32)))
    value_matrix_rows = cast_to_half(jnp.dot(normed, value_weight, preferred_element_type=jnp.float32))
    affinity_logits = jnp.einsum('ljc,ejc->jle', partition_channels(probe_vectors, channel_total).astype(jnp.float32), partition_channels(lookup_vectors, channel_total).astype(jnp.float32))
    softmax_weights = jnp.exp(affinity_logits * (multiplier_list / head_width)[:, None, None])
    totals = lax.optimization_barrier(jnp.sum(softmax_weights, axis=2))
    weighted_values = jnp.einsum('qab,bqg->aqg', cast_to_half(softmax_weights).astype(jnp.float32), partition_channels(value_matrix_rows, channel_total).astype(jnp.float32))
    return (totals, weighted_values.reshape(probe_vectors.shape[0], probe_vectors.shape[1]))

def inducing_finish(totals, weighted_values, anchor, out_weight, up_weight, down_weight, gain_mlp, gain_keys, key_weight, value_weight):
    channel_total = totals.shape[0]
    query_count = weighted_values.shape[0]
    blended = weighted_values.reshape(query_count, channel_total, -1) / jnp.transpose(totals)[:, :, None]
    blended = cast_to_half(blended.reshape(query_count, -1))
    summary = anchor.astype(jnp.float32) + jnp.dot(blended, out_weight, preferred_element_type=jnp.float32)
    hidden = cast_to_half(jax.nn.gelu(jnp.dot(cast_to_half(layer_norm(summary, gain_mlp)), up_weight, preferred_element_type=jnp.float32), approximate=True))
    refined = summary + jnp.dot(hidden, down_weight, preferred_element_type=jnp.float32)
    normed = cast_to_half(layer_norm(refined, gain_keys))
    lookup_vectors = cast_to_half(unit_rms(jnp.dot(normed, key_weight, preferred_element_type=jnp.float32)))
    value_matrix_rows = cast_to_half(jnp.dot(normed, value_weight, preferred_element_type=jnp.float32))
    return (lookup_vectors, value_matrix_rows)

def row_side(current, normed, lookup_vectors, value_matrix_rows, query_weight, out_weight, up_weight, down_weight, gain_mlp, multiplier_list):
    channel_total = multiplier_list.shape[0]
    head_width = lookup_vectors.shape[1] // channel_total
    probe_vectors = cast_to_half(unit_rms(jnp.dot(normed, query_weight, preferred_element_type=jnp.float32)))
    affinity_logits = jnp.einsum('lgu,bgu->lgb', partition_channels(probe_vectors, channel_total).astype(jnp.float32), partition_channels(lookup_vectors, channel_total).astype(jnp.float32))
    softmax_weights = jnp.exp(affinity_logits * (multiplier_list / head_width)[None, :, None])
    softmax_weights = cast_to_half(softmax_weights / lax.optimization_barrier(jnp.sum(softmax_weights, axis=2, keepdims=True)))
    attended_rows = jnp.einsum('gql,lqv->gqv', softmax_weights.astype(jnp.float32), partition_channels(value_matrix_rows, channel_total).astype(jnp.float32))
    attended_rows = cast_to_half(attended_rows.reshape(current.shape[0], -1))
    updated = current.astype(jnp.float32) + jnp.dot(attended_rows, out_weight, preferred_element_type=jnp.float32)
    hidden = cast_to_half(jax.nn.gelu(jnp.dot(cast_to_half(layer_norm(updated, gain_mlp)), up_weight, preferred_element_type=jnp.float32), approximate=True))
    updated = updated + jnp.dot(hidden, down_weight, preferred_element_type=jnp.float32)
    return updated.astype(jnp.bfloat16)

def reference(table_entries, pseudo_points, projection_tensors, expanding_linear, contracting_linear, normalizer_multipliers, sharpness_coefficients):

    def one_column(column):
        current = column
        for stack_position in range(INDUCER_STACKS):
            gain_rows = normalizer_multipliers[stack_position]
            multiplier_list = sharpness_coefficients[stack_position]
            weights_ind = projection_tensors[stack_position, 0]
            weights_row = projection_tensors[stack_position, 1]
            normed = cast_to_half(layer_norm(current, gain_rows[0]))
            probe_vectors = cast_to_half(unit_rms(jnp.dot(pseudo_points[stack_position], weights_ind[0], preferred_element_type=jnp.float32)))
            totals, weighted_values = inducing_partials(normed, probe_vectors, weights_ind[1], weights_ind[2], multiplier_list[0])
            lookup_vectors, value_matrix_rows = inducing_finish(totals, weighted_values, pseudo_points[stack_position], weights_ind[3], expanding_linear[stack_position, 0], contracting_linear[stack_position, 0], gain_rows[2], gain_rows[1], weights_row[1], weights_row[2])
            current = row_side(current, normed, lookup_vectors, value_matrix_rows, weights_row[0], weights_row[3], expanding_linear[stack_position, 1], contracting_linear[stack_position, 1], gain_rows[3], multiplier_list[1])
        return current
    columns = lax.map(one_column, jnp.swapaxes(table_entries, 0, 1))
    return jnp.swapaxes(columns, 0, 1)
```

```python
import functools
import jax
import jax.numpy as jnp
from jax import lax
from jax.experimental import pallas as pl
from jax.sharding import PartitionSpec as P
from jax.experimental.pallas import tpu as pltpu

F32, BF16 = jnp.float32, jnp.bfloat16
LOG2E = 1.4426950408889634
HEADS, HW, E, M = 4, 32, 128, 128
NT = (((1,), (1,)), ((), ()))
RT = 256


def dot(a, b):
    return jnp.dot(a, b, preferred_element_type=F32)


def dot_nt(a, b):
    return lax.dot_general(a, b, NT, preferred_element_type=F32)


def layer_norm(x, gain):
    c = x - jnp.mean(x, axis=-1, keepdims=True)
    v = jnp.mean(c * c, axis=-1, keepdims=True)
    return c * lax.rsqrt(v + 1e-5) * gain


def unit(x):
    return x * lax.rsqrt(jnp.mean(x * x, axis=-1, keepdims=True) + 1e-6)


def gelu(x):
    inner = x * (0.7978845608028654 + (0.7978845608028654 * 0.044715) * (x * x))
    half = 0.5 * x
    return half + half * jnp.tanh(inner)


def head_of_lane(rows):
    return lax.broadcasted_iota(jnp.int32, (rows, E), 1) // HW


def scaled_lanes(values, sharp_row):
    head = head_of_lane(1)
    scale = jnp.zeros((1, E), F32)
    for h in range(HEADS):
        scale = jnp.where(head == h, sharp_row(h) * (LOG2E / HW), scale)
    return values * scale


def spread_heads(values):
    head = head_of_lane(values.shape[0])
    zero = jnp.zeros_like(values)
    return jnp.concatenate([jnp.where(head == h, values, zero) for h in range(HEADS)], axis=0)


def prepare_inducing(b, pseudo, proj, sharp, qbd, wkvq):
    q = unit(dot(pseudo[b], proj[b, 0, 0]))
    q = scaled_lanes(q, lambda h: sharp[b, 0, h]).astype(BF16)
    qbd[...] = spread_heads(q.astype(F32)).astype(BF16)
    wkvq[:, 0:E] = proj[b, 0, 1]
    wkvq[:, E : 2 * E] = proj[b, 0, 2]
    wkvq[:, 2 * E :] = proj[b, 1, 0]


def inducing_rows(x, gain, wkvq, qbd, q_out, p_ref, va_ref, r):
    n = layer_norm(x, gain).astype(BF16)
    kvq = dot(n, wkvq[...])
    k = unit(kvq[:, :E]).astype(BF16)
    q_out[0, pl.ds(r * RT, RT), :] = unit(kvq[:, 2 * E :]).astype(BF16)
    va_ref[pl.ds(r * RT, RT), 0:E] = kvq[:, E : 2 * E].astype(BF16)
    s = dot_nt(qbd[...], k)
    p_ref[:, pl.ds(r * RT, RT)] = jnp.exp2(s).astype(BF16)


def inducing_end(c, cols, p_ref, va_ref, part):
    o = dot(p_ref[...], va_ref[...])
    head = head_of_lane(M)
    lane = lax.broadcasted_iota(jnp.int32, (M, E), 1)
    w = jnp.zeros((M, E), F32)
    pack = part[cols].astype(F32)
    for h in range(HEADS):
        rows = slice(h * M, (h + 1) * M)
        w = jnp.where(head == h, o[rows, :E], w)
        pack = jnp.where(lane == c * HEADS + h, o[rows, E:], pack)
    part[c] = w.astype(BF16)
    part[cols] = pack.astype(BF16)


def finish(b, cols, part, pseudo, proj, up, down, norm, sharp, kbd, vbd, batch):
    gains = norm[b]
    head = head_of_lane(M)
    pack = part(cols)
    for c0 in range(0, cols, batch):
        blended = []
        for c in range(c0, c0 + batch):
            tot = jnp.zeros((M, E), F32)
            for h in range(HEADS):
                col = pack[:, c * HEADS + h : c * HEADS + h + 1]
                tot = jnp.where(head == h, jnp.broadcast_to(col, (M, E)), tot)
            blended.append((part(c) / tot).astype(BF16))
        anchor = jnp.concatenate([pseudo[b].astype(F32)] * batch, axis=0)
        summary = anchor + dot(jnp.concatenate(blended, axis=0), proj[b, 0, 3])
        hidden = gelu(dot(layer_norm(summary, gains[2:3]).astype(BF16), up[b, 0])).astype(BF16)
        refined = summary + dot(hidden, down[b, 0])
        n = layer_norm(refined, gains[1:2]).astype(BF16)
        k = scaled_lanes(unit(dot(n, proj[b, 1, 1])), lambda h: sharp[b, 1, h])
        v = dot(n, proj[b, 1, 2])
        for i in range(batch):
            rows = slice(i * M, (i + 1) * M)
            kbd[c0 + i] = spread_heads(k[rows]).astype(BF16)
            vbd[c0 + i, :, 0:E] = spread_heads(v[rows]).astype(BF16)


def ones_heads():
    return spread_heads(jnp.ones((M, E), F32)).astype(BF16)


def row_rows(b, x, q, kbd_c, vbd_c, proj, up, down, norm):
    s = dot_nt(q, kbd_c)
    p = jnp.exp2(s).astype(BF16)
    o = dot(p, vbd_c)
    att = (o[:, :E] / o[:, E:]).astype(BF16)
    u = x.astype(F32) + dot(att, proj[b, 1, 3])
    n = layer_norm(u, norm[b, 3:4, :]).astype(BF16)
    hidden = gelu(dot(n, up[b, 1])).astype(BF16)
    return (u + dot(hidden, down[b, 1])).astype(BF16)


def first_kernel(cols, t, pseudo, proj, norm, sharp, x_out, q_out, part, xs, qbd, wkvq, p_ref, va_ref):
    c = pl.program_id(0)
    rows = x_out.shape[1]

    @pl.when(c == 0)
    def _():
        prepare_inducing(0, pseudo, proj, sharp, qbd, wkvq)
        va_ref[:, E:] = jnp.ones((rows, E), BF16)
        part[cols] = jnp.zeros((M, E), BF16)
        step = 64

        def widen(i, _):
            block = t[pl.ds(i * step, step)].astype(F32)
            xs[pl.ds(i * step * cols, step * cols), :] = block.reshape(step * cols, E)
            return 0

        lax.fori_loop(0, rows // step, widen, 0)

    for r in range(rows // RT):
        x = xs[pl.ds(c + r * RT * cols, RT, stride=cols), :]
        x_out[0, pl.ds(r * RT, RT), :] = x.astype(BF16)
        inducing_rows(x, norm[0, 0:1, :], wkvq, qbd, q_out, p_ref, va_ref, r)
    inducing_end(c, cols, p_ref, va_ref, part)


def mid_kernel(cols, x_in, q_in, sums, pseudo, proj, up, down, norm, sharp,
               x_out, q_out, part, kbd, vbd, qbd, wkvq, p_ref, va_ref):
    c = pl.program_id(0)
    rows = x_out.shape[1]

    @pl.when(c == 0)
    def _():
        prepare_inducing(1, pseudo, proj, sharp, qbd, wkvq)
        va_ref[:, E:] = jnp.ones((rows, E), BF16)
        part[cols] = jnp.zeros((M, E), BF16)
        for i in range(cols):
            vbd[i, :, E:] = ones_heads()
        finish(0, cols, lambda i: sums[i].astype(F32), pseudo, proj, up, down, norm, sharp, kbd, vbd, 4)

    for r in range(rows // RT):
        at = pl.ds(r * RT, RT)
        y = row_rows(0, x_in[0, at, :], q_in[0, at, :], kbd[c], vbd[c], proj, up, down, norm)
        x_out[0, at, :] = y
        inducing_rows(y.astype(F32), norm[1, 0:1, :], wkvq, qbd, q_out, p_ref, va_ref, r)
    inducing_end(c, cols, p_ref, va_ref, part)


def last_kernel(cols, x_in, q_in, sums, pseudo, proj, up, down, norm, sharp, y_out, ys, kbd, vbd):
    c = pl.program_id(0)
    rows = x_in.shape[1]

    @pl.when(c == 0)
    def _():
        for i in range(cols):
            vbd[i, :, E:] = ones_heads()
        finish(1, cols, lambda i: sums[i].astype(F32), pseudo, proj, up, down, norm, sharp, kbd, vbd, 4)

    for r in range(rows // RT):
        at = pl.ds(r * RT, RT)
        y = row_rows(1, x_in[0, at, :], q_in[0, at, :], kbd[c], vbd[c], proj, up, down, norm)
        ys[pl.ds(c + r * RT * cols, RT, stride=cols), :] = y.astype(F32)

    @pl.when(c == cols - 1)
    def _():
        step = 64

        def narrow(i, _):
            block = ys[pl.ds(i * step * cols, step * cols), :].astype(BF16)
            y_out[pl.ds(i * step, step)] = block.reshape(step, cols, E)
            return 0

        lax.fori_loop(0, rows // step, narrow, 0)


def whole(a):
    return pl.BlockSpec(a.shape, lambda *_: (0,) * a.ndim)


def column(rows):
    return pl.BlockSpec((1, rows, E), lambda c: (c, 0, 0))


SM = pl.BlockSpec(memory_space=pltpu.SMEM)


def shape(dims, dtype=BF16):
    return jax.ShapeDtypeStruct(dims, dtype)


def first(t, pseudo, proj, norm, sharp):
    rows, cols, _ = t.shape
    return pl.pallas_call(
        functools.partial(first_kernel, cols),
        grid=(cols,),
        in_specs=[whole(t), whole(pseudo), whole(proj), whole(norm), SM],
        out_specs=[column(rows), column(rows), pl.BlockSpec((cols + 1, M, E), lambda c: (0, 0, 0))],
        out_shape=[shape((cols, rows, E)), shape((cols, rows, E)), shape((cols + 1, M, E))],
        scratch_shapes=[
            pltpu.VMEM((rows * cols, E), F32),
            pltpu.VMEM((HEADS * M, E), BF16),
            pltpu.VMEM((E, 3 * E), BF16),
            pltpu.VMEM((HEADS * M, rows), BF16),
            pltpu.VMEM((rows, 2 * E), BF16),
        ],
        name="first",
    )(t, pseudo, proj, norm, sharp)


def mid(x, q, sums, pseudo, proj, up, down, norm, sharp):
    cols, rows, _ = x.shape
    return pl.pallas_call(
        functools.partial(mid_kernel, cols),
        grid=(cols,),
        in_specs=[column(rows), column(rows), whole(sums), whole(pseudo), whole(proj), whole(up), whole(down), whole(norm), SM],
        out_specs=[column(rows), column(rows), pl.BlockSpec((cols + 1, M, E), lambda c: (0, 0, 0))],
        out_shape=[shape((cols, rows, E)), shape((cols, rows, E)), shape((cols + 1, M, E))],
        scratch_shapes=[
            pltpu.VMEM((cols, HEADS * M, E), BF16),
            pltpu.VMEM((cols, HEADS * M, 2 * E), BF16),
            pltpu.VMEM((HEADS * M, E), BF16),
            pltpu.VMEM((E, 3 * E), BF16),
            pltpu.VMEM((HEADS * M, rows), BF16),
            pltpu.VMEM((rows, 2 * E), BF16),
        ],
        name="mid",
    )(x, q, sums, pseudo, proj, up, down, norm, sharp)


def last(x, q, sums, pseudo, proj, up, down, norm, sharp):
    cols, rows, _ = x.shape
    return pl.pallas_call(
        functools.partial(last_kernel, cols),
        grid=(cols,),
        in_specs=[column(rows), column(rows), whole(sums), whole(pseudo), whole(proj), whole(up), whole(down), whole(norm), SM],
        out_specs=pl.BlockSpec((rows, cols, E), lambda c: (0, 0, 0)),
        out_shape=shape((rows, cols, E)),
        scratch_shapes=[
            pltpu.VMEM((rows * cols, E), F32),
            pltpu.VMEM((cols, HEADS * M, E), BF16),
            pltpu.VMEM((cols, HEADS * M, 2 * E), BF16),
        ],
        name="last",
    )(x, q, sums, pseudo, proj, up, down, norm, sharp)


def row_sum(part):
    dims = part.shape
    ways = lax.axis_size("row")
    pieces = part.reshape(ways, dims[0] * dims[1] // ways, dims[2])
    pieces = lax.all_to_all(pieces, "row", 0, 0, tiled=True)
    total = jnp.sum(pieces.astype(F32), axis=0).astype(BF16)
    return lax.all_gather(total, "row", axis=0, tiled=True).reshape(dims)


def body(t, pseudo, proj, up, down, norm, sharp):
    x, q, part = first(t, pseudo, proj, norm, sharp)
    x, q, part = mid(x, q, row_sum(part), pseudo, proj, up, down, norm, sharp)
    y = last(x, q, row_sum(part), pseudo, proj, up, down, norm, sharp)
    return lax.all_to_all(y, "feat", split_axis=0, concat_axis=1, tiled=True)


def solution(mesh):
    return jax.shard_map(
        body,
        mesh=mesh,
        in_specs=(P("row", "feat", None), P(), P(), P(), P(), P(), P()),
        out_specs=P(("row", "feat"), None, None),
        check_vma=False,
    )
```

```python
import functools
import jax
import jax.numpy as jnp
from jax import lax
from jax.experimental import pallas as pl
from jax.experimental.pallas import tpu as pltpu
from jax.sharding import PartitionSpec as P

F32, BF16 = jnp.float32, jnp.bfloat16
LOG2E = 1.4426950408889634
HEADS, HW, E, M, FF = 4, 32, 128, 128, 256
NT = (((1,), (1,)), ((), ()))
CB = 4
FB = 8
UNIT = "xlu"
VAR = "xlu"
GELU = "f32"


def dot(a, b):
    return jnp.dot(a, b, preferred_element_type=F32)


def dot_nt(a, b):
    return lax.dot_general(a, b, NT, preferred_element_type=F32)


def layer_norm(x, gain):
    c = x - jnp.mean(x, axis=-1, keepdims=True)
    v = jnp.mean(c * c, axis=-1, keepdims=True)
    return c * lax.rsqrt(v + 1e-5) * gain


def unit(x):
    return x * lax.rsqrt(jnp.mean(x * x, axis=-1, keepdims=True) + 1e-6)


def gelu(x):
    if GELU == "bf16":
        x = x.astype(BF16)
        inner = x * (BF16(0.7978845608028654) + BF16(0.7978845608028654 * 0.044715) * (x * x))
        half = BF16(0.5) * x
        return half + half * jnp.tanh(inner)
    inner = x * (0.7978845608028654 + (0.7978845608028654 * 0.044715) * (x * x))
    half = 0.5 * x
    return (half + half * jnp.tanh(inner)).astype(BF16)


def head_of_lane(rows):
    return lax.broadcasted_iota(jnp.int32, (rows, E), 1) // HW


def averaging():
    return jnp.full((E, E), 1.0 / E, BF16)


def centering():
    eye = lax.broadcasted_iota(jnp.int32, (E, E), 0) == lax.broadcasted_iota(jnp.int32, (E, E), 1)
    return jnp.where(eye, 1.0 - 1.0 / E, -1.0 / E).astype(BF16)


def identity():
    eye = lax.broadcasted_iota(jnp.int32, (E, E), 0) == lax.broadcasted_iota(jnp.int32, (E, E), 1)
    return jnp.where(eye, 1.0, 0.0).astype(BF16)


def as_column(row):
    eye = lax.broadcasted_iota(jnp.int32, (E, E), 0) == lax.broadcasted_iota(jnp.int32, (E, E), 1)
    return jnp.sum(jnp.where(eye, row, 0.0), axis=1, keepdims=True)


def standardized(c, average):
    if VAR == "mxu":
        v = dot((c * c).astype(BF16), average)
    else:
        v = jnp.mean(c * c, axis=-1, keepdims=True)
    return (c * lax.rsqrt(v + 1e-5)).astype(BF16)


def scaled_lanes(values, sharp_row):
    head = head_of_lane(1)
    scale = jnp.zeros((1, E), F32)
    for h in range(HEADS):
        scale = jnp.where(head == h, sharp_row(h) * (LOG2E / HW), scale)
    return values * scale


def spread_heads(values):
    head = head_of_lane(values.shape[0])
    zero = jnp.zeros_like(values)
    return jnp.concatenate([jnp.where(head == h, values, zero) for h in range(HEADS)], axis=0)


def prepare_inducing(b, pseudo, proj, norm, sharp, qbd, wkvq, avg):
    q = unit(dot(pseudo[b], proj[b, 0, 0]))
    q = scaled_lanes(q, lambda h: sharp[b, 0, h])
    qbd[...] = spread_heads(q).astype(BF16)
    gain = as_column(norm[b, 0:1, :])
    wkvq[:, 0:E] = (gain * proj[b, 0, 1].astype(F32)).astype(BF16)
    wkvq[:, E : 2 * E] = (gain * proj[b, 0, 2].astype(F32)).astype(BF16)
    wkvq[:, 2 * E :] = (gain * proj[b, 1, 0].astype(F32)).astype(BF16)
    avg[...] = averaging()


def inducing_block(c0, cols, c, rows, wkvq, qbd, avg, q_out, part):
    n = standardized(c, avg[...])
    kvq = dot(n, wkvq[...])
    k, v, q = kvq[:, :E], kvq[:, E : 2 * E].astype(BF16), kvq[:, 2 * E :]
    if UNIT == "mxu":
        k = k * lax.rsqrt(dot((k * k).astype(BF16), avg[...]) + 1e-6)
        q = q * lax.rsqrt(dot((q * q).astype(BF16), avg[...]) + 1e-6)
    else:
        k, q = unit(k), unit(q)
    k, q = k.astype(BF16), q.astype(BF16)
    q_out[...] = q.reshape(q_out.shape)
    ones = jnp.ones((rows, E), BF16)
    head = head_of_lane(M)
    lane = lax.broadcasted_iota(jnp.int32, (M, E), 1)
    pack = part[cols].astype(F32)
    for i in range(CB):
        at = slice(i * rows, (i + 1) * rows)
        p = jnp.exp2(dot_nt(qbd[...], k[at])).astype(BF16)
        o = dot(p, jnp.concatenate([v[at], ones], axis=1))
        w = jnp.zeros((M, E), F32)
        for h in range(HEADS):
            hr = slice(h * M, (h + 1) * M)
            w = jnp.where(head == h, o[hr, :E], w)
            pack = jnp.where(lane == (c0 + i) * HEADS + h, o[hr, E:], pack)
        part[c0 + i] = w.astype(BF16)
    part[cols] = pack.astype(BF16)


def finish(b, cols, part, pseudo, proj, up, down, norm, sharp, kbd, vbd):
    gains = norm[b]
    head = head_of_lane(M)
    pack = part(cols)
    ones = spread_heads(jnp.ones((M, E), F32)).astype(BF16)
    for c0 in range(0, cols, FB):
        blended = []
        for c in range(c0, c0 + FB):
            tot = jnp.zeros((M, E), F32)
            for h in range(HEADS):
                col = pack[:, c * HEADS + h : c * HEADS + h + 1]
                tot = jnp.where(head == h, jnp.broadcast_to(col, (M, E)), tot)
            blended.append((part(c) / tot).astype(BF16))
        anchor = jnp.concatenate([pseudo[b].astype(F32)] * FB, axis=0)
        summary = anchor + dot(jnp.concatenate(blended, axis=0), proj[b, 0, 3])
        hidden = gelu(dot(layer_norm(summary, gains[2:3]).astype(BF16), up[b, 0]))
        refined = summary + dot(hidden, down[b, 0])
        n = layer_norm(refined, gains[1:2]).astype(BF16)
        k = scaled_lanes(unit(dot(n, proj[b, 1, 1])), lambda h: sharp[b, 1, h])
        v = dot(n, proj[b, 1, 2])
        for i in range(FB):
            rows = slice(i * M, (i + 1) * M)
            kbd[c0 + i] = spread_heads(k[rows]).astype(BF16)
            vbd[c0 + i, :, 0:E] = spread_heads(v[rows]).astype(BF16)
            vbd[c0 + i, :, E:] = ones


def prepare_row(b, proj, up, down, norm, wout, wup, wdown, avg):
    wout[0:E, 0:E] = proj[b, 1, 3]
    wout[0:E, E:] = dot(proj[b, 1, 3], centering()).astype(BF16)
    wout[E:, 0:E] = identity()
    wout[E:, E:] = centering()
    wup[...] = (as_column(norm[b, 3:4, :]) * up[b, 1].astype(F32)).astype(BF16)
    wdown[:, 0:E] = down[b, 1]
    wdown[:, E:] = dot(down[b, 1], centering()).astype(BF16)
    avg[...] = averaging()


def row_block(c0, x, q, rows, kbd, vbd, wout, wup, wdown, avg):
    parts = []
    for i in range(CB):
        p = jnp.exp2(dot_nt(q[i], kbd[c0 + i])).astype(BF16)
        o = dot(p, vbd[c0 + i])
        att = (o[:, :E] / o[:, E:]).astype(BF16)
        parts.append(jnp.concatenate([att, x[i]], axis=1))
    uc = dot(jnp.concatenate(parts, axis=0), wout[...])
    u, c = uc[:, :E], uc[:, E:]
    hidden = gelu(dot(standardized(c, avg[...]), wup[...]))
    yc = dot(hidden, wdown[...])
    return u + yc[:, :E], c + yc[:, E:]


def first_kernel(cols, t, pseudo, proj, norm, sharp, x_out, q_out, part, xs, qbd, wkvq, avg):
    c0 = pl.program_id(0) * CB
    rows = x_out.shape[1]

    @pl.when(c0 == 0)
    def _():
        prepare_inducing(0, pseudo, proj, norm, sharp, qbd, wkvq, avg)
        part[cols] = jnp.zeros((M, E), BF16)
        step = 64

        def widen(i, _):
            block = t[pl.ds(i * step, step)].astype(F32)
            xs[pl.ds(i * step * cols, step * cols), :] = block.reshape(step * cols, E)
            return 0

        lax.fori_loop(0, rows // step, widen, 0)

    x = jnp.concatenate([xs[pl.ds(c0 + i, rows, stride=cols), :].astype(BF16) for i in range(CB)], axis=0)
    x_out[...] = x.reshape(CB, rows, E)
    inducing_block(c0, cols, dot(x, centering()), rows, wkvq, qbd, avg, q_out, part)


def mid_kernel(cols, x_in, q_in, sums, pseudo, proj, up, down, norm, sharp,
               x_out, q_out, part, kbd, vbd, wout, wup, wdown, qbd, wkvq, avg):
    c0 = pl.program_id(0) * CB
    rows = x_out.shape[1]

    @pl.when(c0 == 0)
    def _():
        prepare_row(0, proj, up, down, norm, wout, wup, wdown, avg)
        prepare_inducing(1, pseudo, proj, norm, sharp, qbd, wkvq, avg)
        part[cols] = jnp.zeros((M, E), BF16)
        finish(0, cols, lambda i: sums[i].astype(F32), pseudo, proj, up, down, norm, sharp, kbd, vbd)

    y, c = row_block(c0, x_in, q_in, rows, kbd, vbd, wout, wup, wdown, avg)
    x_out[...] = y.astype(BF16).reshape(CB, rows, E)
    inducing_block(c0, cols, c, rows, wkvq, qbd, avg, q_out, part)


def last_kernel(cols, x_in, q_in, sums, pseudo, proj, up, down, norm, sharp,
                y_out, ys, kbd, vbd, wout, wup, wdown, avg):
    c0 = pl.program_id(0) * CB
    rows = x_in.shape[1]

    @pl.when(c0 == 0)
    def _():
        prepare_row(1, proj, up, down, norm, wout, wup, wdown, avg)
        finish(1, cols, lambda i: sums[i].astype(F32), pseudo, proj, up, down, norm, sharp, kbd, vbd)

    y, _ = row_block(c0, x_in, q_in, rows, kbd, vbd, wout, wup, wdown, avg)
    for i in range(CB):
        ys[pl.ds(c0 + i, rows, stride=cols), :] = y[i * rows : (i + 1) * rows]

    @pl.when(c0 == cols - CB)
    def _():
        step = 64

        def narrow(i, _):
            block = ys[pl.ds(i * step * cols, step * cols), :].astype(BF16)
            y_out[pl.ds(i * step, step)] = block.reshape(step, cols, E)
            return 0

        lax.fori_loop(0, rows // step, narrow, 0)


def whole(a):
    return pl.BlockSpec(a.shape, lambda *_: (0,) * a.ndim)


def column(rows):
    return pl.BlockSpec((CB, rows, E), lambda c: (c, 0, 0))


SM = pl.BlockSpec(memory_space=pltpu.SMEM)


def shape(dims, dtype=BF16):
    return jax.ShapeDtypeStruct(dims, dtype)


def ind_scratch():
    return [pltpu.VMEM((HEADS * M, E), BF16), pltpu.VMEM((E, 3 * E), BF16), pltpu.VMEM((E, E), BF16)]


def row_scratch(cols):
    return [
        pltpu.VMEM((cols, HEADS * M, E), BF16),
        pltpu.VMEM((cols, HEADS * M, 2 * E), BF16),
        pltpu.VMEM((2 * E, 2 * E), BF16),
        pltpu.VMEM((E, FF), BF16),
        pltpu.VMEM((FF, 2 * E), BF16),
    ]


def first(t, pseudo, proj, norm, sharp, group=0, cols=None):
    rows, total, _ = t.shape
    cols = cols or total
    return pl.pallas_call(
        functools.partial(first_kernel, cols),
        grid=(cols // CB,),
        in_specs=[pl.BlockSpec((rows, cols, E), lambda c: (0, group, 0)), whole(pseudo), whole(proj), whole(norm), SM],
        out_specs=[column(rows), column(rows), pl.BlockSpec((cols + 1, M, E), lambda c: (0, 0, 0))],
        out_shape=[shape((cols, rows, E)), shape((cols, rows, E)), shape((cols + 1, M, E))],
        scratch_shapes=[pltpu.VMEM((rows * cols, E), F32), *ind_scratch()],
        name="first",
    )(t, pseudo, proj, norm, sharp)


def mid(x, q, sums, pseudo, proj, up, down, norm, sharp):
    cols, rows, _ = x.shape
    return pl.pallas_call(
        functools.partial(mid_kernel, cols),
        grid=(cols // CB,),
        in_specs=[column(rows), column(rows), whole(sums), whole(pseudo), whole(proj), whole(up), whole(down), whole(norm), SM],
        out_specs=[column(rows), column(rows), pl.BlockSpec((cols + 1, M, E), lambda c: (0, 0, 0))],
        out_shape=[shape((cols, rows, E)), shape((cols, rows, E)), shape((cols + 1, M, E))],
        scratch_shapes=[*row_scratch(cols), *ind_scratch()],
        name="mid",
    )(x, q, sums, pseudo, proj, up, down, norm, sharp)


def last(x, q, sums, pseudo, proj, up, down, norm, sharp):
    cols, rows, _ = x.shape
    return pl.pallas_call(
        functools.partial(last_kernel, cols),
        grid=(cols // CB,),
        in_specs=[column(rows), column(rows), whole(sums), whole(pseudo), whole(proj), whole(up), whole(down), whole(norm), SM],
        out_specs=pl.BlockSpec((rows, cols, E), lambda c: (0, 0, 0)),
        out_shape=shape((rows, cols, E)),
        scratch_shapes=[pltpu.VMEM((rows * cols, E), F32), *row_scratch(cols), pltpu.VMEM((E, E), BF16)],
        name="last",
    )(x, q, sums, pseudo, proj, up, down, norm, sharp)


def row_sum(part):
    dims = part.shape
    ways = lax.axis_size("row")
    pieces = part.reshape(ways, dims[0] * dims[1] // ways, dims[2])
    pieces = lax.all_to_all(pieces, "row", 0, 0, tiled=True)
    total = jnp.sum(pieces.astype(F32), axis=0).astype(BF16)
    copies = jnp.broadcast_to(total, pieces.shape)
    return lax.all_to_all(copies, "row", 0, 0, tiled=True).reshape(dims)


def body(t, pseudo, proj, up, down, norm, sharp):
    x, q, part = first(t, pseudo, proj, norm, sharp)
    x, q, part = mid(x, q, row_sum(part), pseudo, proj, up, down, norm, sharp)
    y = last(x, q, row_sum(part), pseudo, proj, up, down, norm, sharp)
    return lax.all_to_all(y, "feat", split_axis=0, concat_axis=1, tiled=True)


def solution(mesh):
    return jax.shard_map(
        body,
        mesh=mesh,
        in_specs=(P("row", "feat", None), P(), P(), P(), P(), P(), P()),
        out_specs=P(("row", "feat"), None, None),
        check_vma=False,
    )
```

```python
import functools
import jax
import jax.numpy as jnp
from jax import lax
from jax.experimental import pallas as pl
from jax.experimental.pallas import tpu as pltpu
from jax.sharding import PartitionSpec as P

F32, BF16 = jnp.float32, jnp.bfloat16
LOG2E = 1.4426950408889634
HEADS, HW, E, M, FF = 4, 32, 128, 128, 256
NT = (((1,), (1,)), ((), ()))
CB = 4
PV = "t"
WO = "mxu"
OT = "t"
EX = E + 16
FB = 8
UNIT = "xlu"
VAR = "xlu"
GELU = "f32"


def dot(a, b):
    return jnp.dot(a, b, preferred_element_type=F32)


def dot_nt(a, b):
    return lax.dot_general(a, b, NT, preferred_element_type=F32)


def layer_norm(x, gain):
    c = x - jnp.mean(x, axis=-1, keepdims=True)
    v = jnp.mean(c * c, axis=-1, keepdims=True)
    return c * lax.rsqrt(v + 1e-5) * gain


def unit(x):
    return x * lax.rsqrt(jnp.mean(x * x, axis=-1, keepdims=True) + 1e-6)


def gelu(x):
    if GELU == "bf16":
        x = x.astype(BF16)
        inner = x * (BF16(0.7978845608028654) + BF16(0.7978845608028654 * 0.044715) * (x * x))
        half = BF16(0.5) * x
        return half + half * jnp.tanh(inner)
    inner = x * (0.7978845608028654 + (0.7978845608028654 * 0.044715) * (x * x))
    half = 0.5 * x
    return (half + half * jnp.tanh(inner)).astype(BF16)


def head_of_lane(rows):
    return lax.broadcasted_iota(jnp.int32, (rows, E), 1) // HW


def averaging():
    return jnp.full((E, E), 1.0 / E, BF16)


def centering():
    eye = lax.broadcasted_iota(jnp.int32, (E, E), 0) == lax.broadcasted_iota(jnp.int32, (E, E), 1)
    return jnp.where(eye, 1.0 - 1.0 / E, -1.0 / E).astype(BF16)


def identity():
    eye = lax.broadcasted_iota(jnp.int32, (E, E), 0) == lax.broadcasted_iota(jnp.int32, (E, E), 1)
    return jnp.where(eye, 1.0, 0.0).astype(BF16)


def as_column(row):
    eye = lax.broadcasted_iota(jnp.int32, (E, E), 0) == lax.broadcasted_iota(jnp.int32, (E, E), 1)
    return jnp.sum(jnp.where(eye, row, 0.0), axis=1, keepdims=True)


def standardized(c, average):
    if VAR == "mxu":
        v = dot((c * c).astype(BF16), average)
    else:
        v = jnp.mean(c * c, axis=-1, keepdims=True)
    return (c * lax.rsqrt(v + 1e-5)).astype(BF16)


def scaled_lanes(values, sharp_row):
    head = head_of_lane(1)
    scale = jnp.zeros((1, E), F32)
    for h in range(HEADS):
        scale = jnp.where(head == h, sharp_row(h) * (LOG2E / HW), scale)
    return values * scale


def spread_heads(values):
    head = head_of_lane(values.shape[0])
    zero = jnp.zeros_like(values)
    return jnp.concatenate([jnp.where(head == h, values, zero) for h in range(HEADS)], axis=0)


def prepare_inducing(b, pseudo, proj, norm, sharp, qbd, wkvq, wv, avg):
    q = unit(dot(pseudo[b], proj[b, 0, 0]))
    q = scaled_lanes(q, lambda h: sharp[b, 0, h])
    qbd[...] = spread_heads(q).astype(BF16)
    gain = as_column(norm[b, 0:1, :])
    wkvq[:, 0:E] = (gain * proj[b, 0, 1].astype(F32)).astype(BF16)
    wkvq[:, E : 2 * E] = (gain * proj[b, 1, 0].astype(F32)).astype(BF16)
    wv[...] = (jnp.transpose(proj[b, 0, 2].astype(F32)) * norm[b, 0:1, :]).astype(BF16)
    avg[...] = averaging()


def inducing_block(c0, cols, c, rows, wkvq, wv, qbd, avg, q_out, part):
    n = standardized(c, avg[...])
    if PV == "t":
        kq = dot(n, wkvq[:, : 2 * E])
        k, q = unit(kq[:, :E]).astype(BF16), unit(kq[:, E:]).astype(BF16)
        v = dot_nt(wv[...], n).astype(BF16)
        ones = jnp.ones((EX - E, rows), BF16)
    else:
        kvq = dot(n, wkvq[...])
        k, q = unit(kvq[:, :E]).astype(BF16), unit(kvq[:, E : 2 * E]).astype(BF16)
        v = kvq[:, 2 * E :].astype(BF16)
        ones = jnp.ones((rows, E), BF16)
    q_out[...] = q.reshape(q_out.shape)
    head = head_of_lane(M)
    lane = lax.broadcasted_iota(jnp.int32, (M, E), 1)
    totals = []
    for i in range(CB):
        at = slice(i * rows, (i + 1) * rows)
        p = jnp.exp2(dot_nt(qbd[...], k[at])).astype(BF16)
        o = dot_nt(jnp.concatenate([v[:, at], ones], axis=0), p)
        w = [o[h * HW : (h + 1) * HW, h * M : (h + 1) * M] for h in range(HEADS)]
        totals += [o[E : E + 1, h * M : (h + 1) * M] for h in range(HEADS)]
        part[pl.ds(pl.multiple_of((c0 + i) * M, M), M), :] = jnp.concatenate(w, axis=0).astype(BF16)
    at = pl.ds(pl.multiple_of(cols * M + c0 * HEADS, CB * HEADS), CB * HEADS)
    part[at, :] = jnp.concatenate(totals, axis=0).astype(BF16)


def add_up(gathered, sums):
    sums[...] = sum(gathered[i].astype(F32) for i in range(gathered.shape[0]))


def finish(b, cols, sums, pseudo, proj, up, down, norm, sharp, kbd, vbd, vbt):
    gains = norm[b]
    head_s = lax.broadcasted_iota(jnp.int32, (E, M), 0) // HW
    extra = lax.broadcasted_iota(jnp.int32, (EX - E, M), 0)
    ones = spread_heads(jnp.ones((M, E), F32)).astype(BF16)
    for c0 in range(0, cols, FB):
        blended = []
        for c in range(c0, c0 + FB):
            w = sums[c * M : (c + 1) * M, :].astype(F32)
            row = cols * M + c * HEADS // 16 * 16
            tot = sums[row : row + 16, :].astype(F32)
            f = c * HEADS % 16
            pieces = [w[h * HW : (h + 1) * HW] / tot[f + h : f + h + 1] for h in range(HEADS)]
            blended.append(jnp.transpose(jnp.concatenate(pieces, axis=0)).astype(BF16))
        anchor = jnp.concatenate([pseudo[b].astype(F32)] * FB, axis=0)
        summary = anchor + dot(jnp.concatenate(blended, axis=0), proj[b, 0, 3])
        hidden = gelu(dot(layer_norm(summary, gains[2:3]).astype(BF16), up[b, 0]))
        refined = summary + dot(hidden, down[b, 0])
        n = layer_norm(refined, gains[1:2]).astype(BF16)
        k = scaled_lanes(unit(dot(n, proj[b, 1, 1])), lambda h: sharp[b, 1, h])
        v = dot(n, proj[b, 1, 2])
        for i in range(FB):
            rows = slice(i * M, (i + 1) * M)
            kbd[c0 + i] = spread_heads(k[rows]).astype(BF16)
            if OT == "t":
                vt = jnp.transpose(v[rows])
                for h in range(HEADS):
                    lanes = slice(h * M, (h + 1) * M)
                    vbt[c0 + i, 0:E, lanes] = jnp.where(head_s == h, vt, 0.0).astype(BF16)
                    vbt[c0 + i, E:, lanes] = jnp.where(extra == h, 1.0, 0.0).astype(BF16)
            else:
                vbd[c0 + i, :, 0:E] = spread_heads(v[rows]).astype(BF16)
                vbd[c0 + i, :, E:] = ones


def prepare_row(b, proj, up, down, norm, wout, wup, wdown, avg):
    wout[0:E, 0:E] = proj[b, 1, 3]
    wout[0:E, E:] = dot(proj[b, 1, 3], centering()).astype(BF16)
    wout[E:, 0:E] = identity()
    wout[E:, E:] = centering()
    wup[...] = (as_column(norm[b, 3:4, :]) * up[b, 1].astype(F32)).astype(BF16)
    wdown[:, 0:E] = down[b, 1]
    wdown[:, E:] = dot(down[b, 1], centering()).astype(BF16)
    avg[...] = averaging()


def row_block(c0, x, q, rows, kbd, vbd, vbt, wout, wup, wdown, avg):
    parts = []
    for i in range(CB):
        if OT == "t":
            p = jnp.exp2(dot_nt(kbd[c0 + i], q[i])).astype(BF16)
            o = dot(vbt[c0 + i], p)
            over = 1.0 / o[E : E + 8]
            att = [o[h * HW : (h + 1) * HW] * over[h : h + 1] for h in range(HEADS)]
            att = jnp.transpose(jnp.concatenate(att, axis=0)).astype(BF16)
        else:
            p = jnp.exp2(dot_nt(q[i], kbd[c0 + i])).astype(BF16)
            o = dot(p, vbd[c0 + i])
            att = (o[:, :E] / o[:, E:]).astype(BF16)
        parts.append(jnp.concatenate([att, x[i]], axis=1) if WO == "mxu" else att)
    if WO == "mxu":
        uc = dot(jnp.concatenate(parts, axis=0), wout[...])
        u, c = uc[:, :E], uc[:, E:]
    else:
        u = x[...].reshape(CB * rows, E).astype(F32) + dot(jnp.concatenate(parts, axis=0), wout[0:E, 0:E])
        c = u - jnp.mean(u, axis=-1, keepdims=True)
    hidden = gelu(dot(standardized(c, avg[...]), wup[...]))
    yc = dot(hidden, wdown[...])
    return u + yc[:, :E], c + yc[:, E:]


def first_kernel(cols, t, pseudo, proj, norm, sharp, x_out, q_out, part, xs, qbd, wkvq, wv, avg):
    c0 = pl.program_id(0) * CB
    rows = x_out.shape[1]

    @pl.when(c0 == 0)
    def _():
        prepare_inducing(0, pseudo, proj, norm, sharp, qbd, wkvq, wv, avg)
        part[cols * M :, :] = jnp.zeros((part.shape[0] - cols * M, E), BF16)
        step = 64

        def widen(i, _):
            block = t[pl.ds(i * step, step)].astype(F32)
            xs[pl.ds(i * step * cols, step * cols), :] = block.reshape(step * cols, E)
            return 0

        lax.fori_loop(0, rows // step, widen, 0)

    x = jnp.concatenate([xs[pl.ds(c0 + i, rows, stride=cols), :].astype(BF16) for i in range(CB)], axis=0)
    x_out[...] = x.reshape(CB, rows, E)
    inducing_block(c0, cols, dot(x, centering()), rows, wkvq, wv, qbd, avg, q_out, part)


def mid_kernel(cols, x_in, q_in, gathered, pseudo, proj, up, down, norm, sharp,
               x_out, q_out, part, sums, kbd, vbd, vbt, wout, wup, wdown, qbd, wkvq, wv, avg):
    c0 = pl.program_id(0) * CB
    rows = x_out.shape[1]

    @pl.when(c0 == 0)
    def _():
        prepare_row(0, proj, up, down, norm, wout, wup, wdown, avg)
        prepare_inducing(1, pseudo, proj, norm, sharp, qbd, wkvq, wv, avg)
        part[cols * M :, :] = jnp.zeros((part.shape[0] - cols * M, E), BF16)
        add_up(gathered, sums)
        finish(0, cols, sums, pseudo, proj, up, down, norm, sharp, kbd, vbd, vbt)

    y, c = row_block(c0, x_in, q_in, rows, kbd, vbd, vbt, wout, wup, wdown, avg)
    x_out[...] = y.astype(BF16).reshape(CB, rows, E)
    inducing_block(c0, cols, c, rows, wkvq, wv, qbd, avg, q_out, part)


def last_kernel(cols, x_in, q_in, gathered, pseudo, proj, up, down, norm, sharp,
                y_out, ys, sums, kbd, vbd, vbt, wout, wup, wdown, avg):
    c0 = pl.program_id(0) * CB
    rows = x_in.shape[1]

    @pl.when(c0 == 0)
    def _():
        prepare_row(1, proj, up, down, norm, wout, wup, wdown, avg)
        add_up(gathered, sums)
        finish(1, cols, sums, pseudo, proj, up, down, norm, sharp, kbd, vbd, vbt)

    y, _ = row_block(c0, x_in, q_in, rows, kbd, vbd, vbt, wout, wup, wdown, avg)
    for i in range(CB):
        ys[pl.ds(c0 + i, rows, stride=cols), :] = y[i * rows : (i + 1) * rows]

    @pl.when(c0 == cols - CB)
    def _():
        step = 64

        def narrow(i, _):
            block = ys[pl.ds(i * step * cols, step * cols), :].astype(BF16)
            y_out[pl.ds(i * step, step)] = block.reshape(step, cols, E)
            return 0

        lax.fori_loop(0, rows // step, narrow, 0)


def whole(a):
    return pl.BlockSpec(a.shape, lambda *_: (0,) * a.ndim)


def column(rows):
    return pl.BlockSpec((CB, rows, E), lambda c: (c, 0, 0))


SM = pl.BlockSpec(memory_space=pltpu.SMEM)


def shape(dims, dtype=BF16):
    return jax.ShapeDtypeStruct(dims, dtype)


def ind_scratch():
    return [pltpu.VMEM((HEADS * M, E), BF16), pltpu.VMEM((E, 2 * E), BF16), pltpu.VMEM((E, E), BF16), pltpu.VMEM((E, E), BF16)]


def row_scratch(cols, size):
    return [
        pltpu.VMEM((size, E), F32),
        pltpu.VMEM((cols, HEADS * M, E), BF16),
        pltpu.VMEM((cols, HEADS * M, 2 * E), BF16),
        pltpu.VMEM((cols, EX, HEADS * M), BF16),
        pltpu.VMEM((2 * E, 2 * E), BF16),
        pltpu.VMEM((E, FF), BF16),
        pltpu.VMEM((FF, 2 * E), BF16),
    ]


def first(t, pseudo, proj, norm, sharp, group, cols, size):
    rows, total, _ = t.shape
    return pl.pallas_call(
        functools.partial(first_kernel, cols),
        grid=(cols // CB,),
        in_specs=[pl.BlockSpec((rows, cols, E), lambda c: (0, group, 0)), whole(pseudo), whole(proj), whole(norm), SM],
        out_specs=[column(rows), column(rows), pl.BlockSpec((size, E), lambda c: (0, 0))],
        out_shape=[shape((cols, rows, E)), shape((cols, rows, E)), shape((size, E))],
        scratch_shapes=[pltpu.VMEM((rows * cols, E), F32), *ind_scratch()],
        name="first",
    )(t, pseudo, proj, norm, sharp)


def mid(x, q, sums, pseudo, proj, up, down, norm, sharp, size):
    cols, rows, _ = x.shape
    return pl.pallas_call(
        functools.partial(mid_kernel, cols),
        grid=(cols // CB,),
        in_specs=[column(rows), column(rows), whole(sums), whole(pseudo), whole(proj), whole(up), whole(down), whole(norm), SM],
        out_specs=[column(rows), column(rows), pl.BlockSpec((size, E), lambda c: (0, 0))],
        out_shape=[shape((cols, rows, E)), shape((cols, rows, E)), shape((size, E))],
        scratch_shapes=[*row_scratch(cols, sums.shape[1]), *ind_scratch()],
        name="mid",
    )(x, q, sums, pseudo, proj, up, down, norm, sharp)


def last(x, q, sums, pseudo, proj, up, down, norm, sharp):
    cols, rows, _ = x.shape
    return pl.pallas_call(
        functools.partial(last_kernel, cols),
        grid=(cols // CB,),
        in_specs=[column(rows), column(rows), whole(sums), whole(pseudo), whole(proj), whole(up), whole(down), whole(norm), SM],
        out_specs=pl.BlockSpec((rows, cols, E), lambda c: (0, 0, 0)),
        out_shape=shape((rows, cols, E)),
        scratch_shapes=[pltpu.VMEM((rows * cols, E), F32), *row_scratch(cols, sums.shape[1]), pltpu.VMEM((E, E), BF16)],
        name="last",
    )(x, q, sums, pseudo, proj, up, down, norm, sharp)


def gathered_parts(part):
    return lax.all_gather(part, "row")


def body(t, pseudo, proj, up, down, norm, sharp):
    feat = lax.axis_size("feat")
    rows, total, _ = t.shape
    groups = 2
    cols = total // groups
    size = cols * (M + HEADS)
    a = [first(t, pseudo, proj, norm, sharp, g, cols, size) for g in range(groups)]
    a = [(x, q, gathered_parts(part)) for x, q, part in a]
    a = [mid(x, q, s, pseudo, proj, up, down, norm, sharp, size) for x, q, s in a]
    a = [(x, q, gathered_parts(part)) for x, q, part in a]
    y = [last(x, q, s, pseudo, proj, up, down, norm, sharp) for x, q, s in a]
    y = [lax.all_to_all(v.reshape(feat, rows // feat, cols, E), "feat", 0, 0, tiled=True) for v in y]
    y = jnp.stack(y, axis=2)
    return jnp.transpose(y, (1, 0, 2, 3, 4)).reshape(rows // feat, feat * total, E)


def solution(mesh):
    return jax.shard_map(
        body,
        mesh=mesh,
        in_specs=(P("row", "feat", None), P(), P(), P(), P(), P(), P()),
        out_specs=P(("row", "feat"), None, None),
        check_vma=False,
    )
```

```python
import functools
import jax
import jax.numpy as jnp
from jax import lax
from jax.experimental import pallas as pl
from jax.experimental.pallas import tpu as pltpu
from jax.sharding import PartitionSpec as P

F32, BF16 = jnp.float32, jnp.bfloat16
LOG2E = 1.4426950408889634
HEADS, HW, E, M, FF = 4, 32, 128, 128, 256
NT = (((1,), (1,)), ((), ()))
CB = 2
PV = "t"
WO = "mxu"
OT = "t"
EX = E + 16
FB = 8
UNIT = "xlu"
VAR = "xlu"
GELU = "f32"


def dot(a, b):
    return jnp.dot(a, b, preferred_element_type=F32)


def dot_nt(a, b):
    return lax.dot_general(a, b, NT, preferred_element_type=F32)


def layer_norm(x, gain):
    c = x - jnp.mean(x, axis=-1, keepdims=True)
    v = jnp.mean(c * c, axis=-1, keepdims=True)
    return c * lax.rsqrt(v + 1e-5) * gain


def unit(x):
    return x * lax.rsqrt(jnp.mean(x * x, axis=-1, keepdims=True) + 1e-6)


def gelu(x):
    if GELU == "bf16":
        x = x.astype(BF16)
        inner = x * (BF16(0.7978845608028654) + BF16(0.7978845608028654 * 0.044715) * (x * x))
        half = BF16(0.5) * x
        return half + half * jnp.tanh(inner)
    inner = x * (0.7978845608028654 + (0.7978845608028654 * 0.044715) * (x * x))
    half = 0.5 * x
    return (half + half * jnp.tanh(inner)).astype(BF16)


def head_of_lane(rows):
    return lax.broadcasted_iota(jnp.int32, (rows, E), 1) // HW


def averaging():
    return jnp.full((E, E), 1.0 / E, BF16)


def centering():
    eye = lax.broadcasted_iota(jnp.int32, (E, E), 0) == lax.broadcasted_iota(jnp.int32, (E, E), 1)
    return jnp.where(eye, 1.0 - 1.0 / E, -1.0 / E).astype(BF16)


def identity():
    eye = lax.broadcasted_iota(jnp.int32, (E, E), 0) == lax.broadcasted_iota(jnp.int32, (E, E), 1)
    return jnp.where(eye, 1.0, 0.0).astype(BF16)


def as_column(row):
    eye = lax.broadcasted_iota(jnp.int32, (E, E), 0) == lax.broadcasted_iota(jnp.int32, (E, E), 1)
    return jnp.sum(jnp.where(eye, row, 0.0), axis=1, keepdims=True)


def standardized(c, average):
    if VAR == "mxu":
        v = dot((c * c).astype(BF16), average)
    else:
        v = jnp.mean(c * c, axis=-1, keepdims=True)
    return (c * lax.rsqrt(v + 1e-5)).astype(BF16)


def scaled_lanes(values, sharp_row):
    head = head_of_lane(1)
    scale = jnp.zeros((1, E), F32)
    for h in range(HEADS):
        scale = jnp.where(head == h, sharp_row(h) * (LOG2E / HW), scale)
    return values * scale


def spread_heads(values):
    head = head_of_lane(values.shape[0])
    zero = jnp.zeros_like(values)
    return jnp.concatenate([jnp.where(head == h, values, zero) for h in range(HEADS)], axis=0)


def prepare_inducing(b, pseudo, proj, norm, sharp, qbd, wkvq, wv, avg):
    q = unit(dot(pseudo[b], proj[b, 0, 0]))
    q = scaled_lanes(q, lambda h: sharp[b, 0, h])
    qbd[...] = spread_heads(q).astype(BF16)
    gain = as_column(norm[b, 0:1, :])
    wkvq[:, 0:E] = (gain * proj[b, 0, 1].astype(F32)).astype(BF16)
    wkvq[:, E : 2 * E] = (gain * proj[b, 1, 0].astype(F32)).astype(BF16)
    wv[...] = (jnp.transpose(proj[b, 0, 2].astype(F32)) * norm[b, 0:1, :]).astype(BF16)
    avg[...] = averaging()


def inducing_block(c0, cols, c, rows, wkvq, wv, qbd, avg, q_out, part):
    n = standardized(c, avg[...])
    if PV == "t":
        kq = dot(n, wkvq[:, : 2 * E])
        k, q = unit(kq[:, :E]).astype(BF16), unit(kq[:, E:]).astype(BF16)
        v = dot_nt(wv[...], n).astype(BF16)
        ones = jnp.ones((EX - E, rows), BF16)
    else:
        kvq = dot(n, wkvq[...])
        k, q = unit(kvq[:, :E]).astype(BF16), unit(kvq[:, E : 2 * E]).astype(BF16)
        v = kvq[:, 2 * E :].astype(BF16)
        ones = jnp.ones((rows, E), BF16)
    q_out[...] = q.reshape(q_out.shape)
    head = head_of_lane(M)
    lane = lax.broadcasted_iota(jnp.int32, (M, E), 1)
    totals = []
    for i in range(CB):
        at = slice(i * rows, (i + 1) * rows)
        p = jnp.exp2(dot_nt(qbd[...], k[at])).astype(BF16)
        o = dot_nt(jnp.concatenate([v[:, at], ones], axis=0), p)
        w = [o[h * HW : (h + 1) * HW, h * M : (h + 1) * M] for h in range(HEADS)]
        totals += [o[E : E + 1, h * M : (h + 1) * M] for h in range(HEADS)]
        part[pl.ds(pl.multiple_of((c0 + i) * M, M), M), :] = jnp.concatenate(w, axis=0).astype(BF16)
    at = pl.ds(pl.multiple_of(cols * M + c0 * HEADS, CB * HEADS), CB * HEADS)
    part[at, :] = jnp.concatenate(totals, axis=0).astype(BF16)


def add_up(gathered, sums):
    sums[...] = sum(gathered[i].astype(F32) for i in range(gathered.shape[0]))


def finish(b, cols, sums, pseudo, proj, up, down, norm, sharp, kbd, vbd, vbt):
    gains = norm[b]
    head_s = lax.broadcasted_iota(jnp.int32, (E, M), 0) // HW
    extra = lax.broadcasted_iota(jnp.int32, (EX - E, M), 0)
    ones = spread_heads(jnp.ones((M, E), F32)).astype(BF16)
    for c0 in range(0, cols, FB):
        blended = []
        for c in range(c0, c0 + FB):
            w = sums[c * M : (c + 1) * M, :].astype(F32)
            row = cols * M + c * HEADS // 16 * 16
            tot = sums[row : row + 16, :].astype(F32)
            f = c * HEADS % 16
            pieces = [w[h * HW : (h + 1) * HW] / tot[f + h : f + h + 1] for h in range(HEADS)]
            blended.append(jnp.transpose(jnp.concatenate(pieces, axis=0)).astype(BF16))
        anchor = jnp.concatenate([pseudo[b].astype(F32)] * FB, axis=0)
        summary = anchor + dot(jnp.concatenate(blended, axis=0), proj[b, 0, 3])
        hidden = gelu(dot(layer_norm(summary, gains[2:3]).astype(BF16), up[b, 0]))
        refined = summary + dot(hidden, down[b, 0])
        n = layer_norm(refined, gains[1:2]).astype(BF16)
        k = scaled_lanes(unit(dot(n, proj[b, 1, 1])), lambda h: sharp[b, 1, h])
        v = dot(n, proj[b, 1, 2])
        for i in range(FB):
            rows = slice(i * M, (i + 1) * M)
            kbd[c0 + i] = spread_heads(k[rows]).astype(BF16)
            if OT == "t":
                vt = jnp.transpose(v[rows])
                for h in range(HEADS):
                    lanes = slice(h * M, (h + 1) * M)
                    vbt[c0 + i, 0:E, lanes] = jnp.where(head_s == h, vt, 0.0).astype(BF16)
                    vbt[c0 + i, E:, lanes] = jnp.where(extra == h, 1.0, 0.0).astype(BF16)
            else:
                vbd[c0 + i, :, 0:E] = spread_heads(v[rows]).astype(BF16)
                vbd[c0 + i, :, E:] = ones


def prepare_row(b, proj, up, down, norm, wout, wup, wdown, avg):
    wout[0:E, 0:E] = proj[b, 1, 3]
    wout[0:E, E:] = dot(proj[b, 1, 3], centering()).astype(BF16)
    wout[E:, 0:E] = identity()
    wout[E:, E:] = centering()
    wup[...] = (as_column(norm[b, 3:4, :]) * up[b, 1].astype(F32)).astype(BF16)
    wdown[:, 0:E] = down[b, 1]
    wdown[:, E:] = dot(down[b, 1], centering()).astype(BF16)
    avg[...] = averaging()


def row_block(c0, x, q, rows, kbd, vbd, vbt, wout, wup, wdown, avg):
    parts = []
    for i in range(CB):
        if OT == "t":
            p = jnp.exp2(dot_nt(kbd[c0 + i], q[i])).astype(BF16)
            o = dot(vbt[c0 + i], p)
            over = 1.0 / o[E : E + 8]
            att = [o[h * HW : (h + 1) * HW] * over[h : h + 1] for h in range(HEADS)]
            att = jnp.transpose(jnp.concatenate(att, axis=0)).astype(BF16)
        else:
            p = jnp.exp2(dot_nt(q[i], kbd[c0 + i])).astype(BF16)
            o = dot(p, vbd[c0 + i])
            att = (o[:, :E] / o[:, E:]).astype(BF16)
        parts.append(jnp.concatenate([att, x[i]], axis=1) if WO == "mxu" else att)
    if WO == "mxu":
        uc = dot(jnp.concatenate(parts, axis=0), wout[...])
        u, c = uc[:, :E], uc[:, E:]
    else:
        u = x[...].reshape(CB * rows, E).astype(F32) + dot(jnp.concatenate(parts, axis=0), wout[0:E, 0:E])
        c = u - jnp.mean(u, axis=-1, keepdims=True)
    hidden = gelu(dot(standardized(c, avg[...]), wup[...]))
    yc = dot(hidden, wdown[...])
    return u + yc[:, :E], c + yc[:, E:]


def first_kernel(cols, t, pseudo, proj, norm, sharp, x_out, q_out, part, xs, qbd, wkvq, wv, avg):
    c0 = pl.program_id(0) * CB
    rows = x_out.shape[1]

    @pl.when(c0 == 0)
    def _():
        prepare_inducing(0, pseudo, proj, norm, sharp, qbd, wkvq, wv, avg)
        part[cols * M :, :] = jnp.zeros((part.shape[0] - cols * M, E), BF16)
        step = 64

        def widen(i, _):
            block = t[pl.ds(i * step, step)].astype(F32)
            xs[pl.ds(i * step * cols, step * cols), :] = block.reshape(step * cols, E)
            return 0

        lax.fori_loop(0, rows // step, widen, 0)

    x = jnp.concatenate([xs[pl.ds(c0 + i, rows, stride=cols), :].astype(BF16) for i in range(CB)], axis=0)
    x_out[...] = x.reshape(CB, rows, E)
    inducing_block(c0, cols, dot(x, centering()), rows, wkvq, wv, qbd, avg, q_out, part)


def mid_kernel(cols, x_in, q_in, gathered, pseudo, proj, up, down, norm, sharp,
               x_out, q_out, part, sums, kbd, vbd, vbt, wout, wup, wdown, qbd, wkvq, wv, avg):
    c0 = pl.program_id(0) * CB
    rows = x_out.shape[1]

    @pl.when(c0 == 0)
    def _():
        prepare_row(0, proj, up, down, norm, wout, wup, wdown, avg)
        prepare_inducing(1, pseudo, proj, norm, sharp, qbd, wkvq, wv, avg)
        part[cols * M :, :] = jnp.zeros((part.shape[0] - cols * M, E), BF16)
        add_up(gathered, sums)
        finish(0, cols, sums, pseudo, proj, up, down, norm, sharp, kbd, vbd, vbt)

    y, c = row_block(c0, x_in, q_in, rows, kbd, vbd, vbt, wout, wup, wdown, avg)
    x_out[...] = y.astype(BF16).reshape(CB, rows, E)
    inducing_block(c0, cols, c, rows, wkvq, wv, qbd, avg, q_out, part)


def last_kernel(cols, x_in, q_in, gathered, pseudo, proj, up, down, norm, sharp,
                y_out, ys, sums, kbd, vbd, vbt, wout, wup, wdown, avg):
    c0 = pl.program_id(0) * CB
    rows = x_in.shape[1]

    @pl.when(c0 == 0)
    def _():
        prepare_row(1, proj, up, down, norm, wout, wup, wdown, avg)
        add_up(gathered, sums)
        finish(1, cols, sums, pseudo, proj, up, down, norm, sharp, kbd, vbd, vbt)

    y, _ = row_block(c0, x_in, q_in, rows, kbd, vbd, vbt, wout, wup, wdown, avg)
    for i in range(CB):
        ys[pl.ds(c0 + i, rows, stride=cols), :] = y[i * rows : (i + 1) * rows]

    @pl.when(c0 == cols - CB)
    def _():
        step = 64

        def narrow(i, _):
            block = ys[pl.ds(i * step * cols, step * cols), :].astype(BF16)
            y_out[pl.ds(i * step, step)] = block.reshape(step, cols, E)
            return 0

        lax.fori_loop(0, rows // step, narrow, 0)


def whole(a):
    return pl.BlockSpec(a.shape, lambda *_: (0,) * a.ndim)


def column(rows):
    return pl.BlockSpec((CB, rows, E), lambda c: (c, 0, 0))


SM = pl.BlockSpec(memory_space=pltpu.SMEM)


def shape(dims, dtype=BF16):
    return jax.ShapeDtypeStruct(dims, dtype)


def ind_scratch():
    return [pltpu.VMEM((HEADS * M, E), BF16), pltpu.VMEM((E, 2 * E), BF16), pltpu.VMEM((E, E), BF16), pltpu.VMEM((E, E), BF16)]


def row_scratch(cols, size):
    return [
        pltpu.VMEM((size, E), F32),
        pltpu.VMEM((cols, HEADS * M, E), BF16),
        pltpu.VMEM((cols, HEADS * M, 2 * E), BF16),
        pltpu.VMEM((cols, EX, HEADS * M), BF16),
        pltpu.VMEM((2 * E, 2 * E), BF16),
        pltpu.VMEM((E, FF), BF16),
        pltpu.VMEM((FF, 2 * E), BF16),
    ]


def first(t, pseudo, proj, norm, sharp, group, cols, size):
    rows, total, _ = t.shape
    return pl.pallas_call(
        functools.partial(first_kernel, cols),
        grid=(cols // CB,),
        in_specs=[pl.BlockSpec((rows, cols, E), lambda c: (0, group, 0)), whole(pseudo), whole(proj), whole(norm), SM],
        out_specs=[column(rows), column(rows), pl.BlockSpec((size, E), lambda c: (0, 0))],
        out_shape=[shape((cols, rows, E)), shape((cols, rows, E)), shape((size, E))],
        scratch_shapes=[pltpu.VMEM((rows * cols, E), F32), *ind_scratch()],
        name="first",
    )(t, pseudo, proj, norm, sharp)


def mid(x, q, sums, pseudo, proj, up, down, norm, sharp, size):
    cols, rows, _ = x.shape
    return pl.pallas_call(
        functools.partial(mid_kernel, cols),
        grid=(cols // CB,),
        in_specs=[column(rows), column(rows), whole(sums), whole(pseudo), whole(proj), whole(up), whole(down), whole(norm), SM],
        out_specs=[column(rows), column(rows), pl.BlockSpec((size, E), lambda c: (0, 0))],
        out_shape=[shape((cols, rows, E)), shape((cols, rows, E)), shape((size, E))],
        scratch_shapes=[*row_scratch(cols, sums.shape[1]), *ind_scratch()],
        name="mid",
    )(x, q, sums, pseudo, proj, up, down, norm, sharp)


def last(x, q, sums, pseudo, proj, up, down, norm, sharp):
    cols, rows, _ = x.shape
    return pl.pallas_call(
        functools.partial(last_kernel, cols),
        grid=(cols // CB,),
        in_specs=[column(rows), column(rows), whole(sums), whole(pseudo), whole(proj), whole(up), whole(down), whole(norm), SM],
        out_specs=pl.BlockSpec((rows, cols, E), lambda c: (0, 0, 0)),
        out_shape=shape((rows, cols, E)),
        scratch_shapes=[pltpu.VMEM((rows * cols, E), F32), *row_scratch(cols, sums.shape[1]), pltpu.VMEM((E, E), BF16)],
        name="last",
    )(x, q, sums, pseudo, proj, up, down, norm, sharp)


def gathered_parts(part):
    return lax.all_gather(part, "row")


def body(t, pseudo, proj, up, down, norm, sharp):
    feat = lax.axis_size("feat")
    rows, total, _ = t.shape
    groups = 2
    cols = total // groups
    size = cols * (M + HEADS)
    a = [first(t, pseudo, proj, norm, sharp, g, cols, size) for g in range(groups)]
    a = [(x, q, gathered_parts(part)) for x, q, part in a]
    a = [mid(x, q, s, pseudo, proj, up, down, norm, sharp, size) for x, q, s in a]
    a = [(x, q, gathered_parts(part)) for x, q, part in a]
    y = [last(x, q, s, pseudo, proj, up, down, norm, sharp) for x, q, s in a]
    y = [lax.all_to_all(v.reshape(feat, rows // feat, cols, E), "feat", 0, 0, tiled=True) for v in y]
    y = jnp.stack(y, axis=2)
    return jnp.transpose(y, (1, 0, 2, 3, 4)).reshape(rows // feat, feat * total, E)


def solution(mesh):
    return jax.shard_map(
        body,
        mesh=mesh,
        in_specs=(P("row", "feat", None), P(), P(), P(), P(), P(), P()),
        out_specs=P(("row", "feat"), None, None),
        check_vma=False,
    )
```

```python
import functools
import jax
import jax.numpy as jnp
from jax import lax
from jax.experimental import pallas as pl
from jax.experimental.pallas import tpu as pltpu
from jax.sharding import PartitionSpec as P

F32, BF16 = jnp.float32, jnp.bfloat16
LOG2E = 1.4426950408889634
HEADS, HW, E, M, FF = 4, 32, 128, 128, 256
NT = (((1,), (1,)), ((), ()))
CB = 2
PV = "t"
WO = "mxu"
OT = "t"
EX = E + 16
FB = 8
UNIT = "xlu"
VAR = "xlu"
GELU = "f32"


def dot(a, b):
    return jnp.dot(a, b, preferred_element_type=F32)


def dot_nt(a, b):
    return lax.dot_general(a, b, NT, preferred_element_type=F32)


def layer_norm(x, gain):
    c = x - jnp.mean(x, axis=-1, keepdims=True)
    v = jnp.mean(c * c, axis=-1, keepdims=True)
    return c * lax.rsqrt(v + 1e-5) * gain


def unit(x):
    return x * lax.rsqrt(jnp.mean(x * x, axis=-1, keepdims=True) + 1e-6)


def gelu(x):
    if GELU == "bf16":
        x = x.astype(BF16)
        inner = x * (BF16(0.7978845608028654) + BF16(0.7978845608028654 * 0.044715) * (x * x))
        half = BF16(0.5) * x
        return half + half * jnp.tanh(inner)
    inner = x * (0.7978845608028654 + (0.7978845608028654 * 0.044715) * (x * x))
    half = 0.5 * x
    return (half + half * jnp.tanh(inner)).astype(BF16)


def head_of_lane(rows):
    return lax.broadcasted_iota(jnp.int32, (rows, E), 1) // HW


def averaging():
    return jnp.full((E, E), 1.0 / E, BF16)


def centering():
    eye = lax.broadcasted_iota(jnp.int32, (E, E), 0) == lax.broadcasted_iota(jnp.int32, (E, E), 1)
    return jnp.where(eye, 1.0 - 1.0 / E, -1.0 / E).astype(BF16)


def identity():
    eye = lax.broadcasted_iota(jnp.int32, (E, E), 0) == lax.broadcasted_iota(jnp.int32, (E, E), 1)
    return jnp.where(eye, 1.0, 0.0).astype(BF16)


def as_column(row):
    eye = lax.broadcasted_iota(jnp.int32, (E, E), 0) == lax.broadcasted_iota(jnp.int32, (E, E), 1)
    return jnp.sum(jnp.where(eye, row, 0.0), axis=1, keepdims=True)


def standardized(c, average):
    if VAR == "mxu":
        v = dot((c * c).astype(BF16), average)
    else:
        v = jnp.mean(c * c, axis=-1, keepdims=True)
    return (c * lax.rsqrt(v + 1e-5)).astype(BF16)


def scaled_lanes(values, sharp_row):
    head = head_of_lane(1)
    scale = jnp.zeros((1, E), F32)
    for h in range(HEADS):
        scale = jnp.where(head == h, sharp_row(h) * (LOG2E / HW), scale)
    return values * scale


def spread_heads(values):
    head = head_of_lane(values.shape[0])
    zero = jnp.zeros_like(values)
    return jnp.concatenate([jnp.where(head == h, values, zero) for h in range(HEADS)], axis=0)


def prepare_inducing(b, pseudo, proj, norm, sharp, qbd, wkvq, wv, avg):
    q = unit(dot(pseudo[b], proj[b, 0, 0]))
    q = scaled_lanes(q, lambda h: sharp[b, 0, h])
    qbd[...] = spread_heads(q).astype(BF16)
    gain = as_column(norm[b, 0:1, :])
    wkvq[:, 0:E] = (gain * proj[b, 0, 1].astype(F32)).astype(BF16)
    wkvq[:, E : 2 * E] = (gain * proj[b, 1, 0].astype(F32)).astype(BF16)
    wv[...] = (jnp.transpose(proj[b, 0, 2].astype(F32)) * norm[b, 0:1, :]).astype(BF16)
    avg[...] = averaging()


def inducing_block(c0, cols, c, rows, wkvq, wv, qbd, avg, q_out, part):
    n = standardized(c, avg[...])
    if PV == "t":
        kq = dot(n, wkvq[:, : 2 * E])
        k, q = unit(kq[:, :E]).astype(BF16), unit(kq[:, E:]).astype(BF16)
        v = dot_nt(wv[...], n).astype(BF16)
        ones = jnp.ones((EX - E, rows), BF16)
    else:
        kvq = dot(n, wkvq[...])
        k, q = unit(kvq[:, :E]).astype(BF16), unit(kvq[:, E : 2 * E]).astype(BF16)
        v = kvq[:, 2 * E :].astype(BF16)
        ones = jnp.ones((rows, E), BF16)
    q_out[...] = q.reshape(q_out.shape)
    head = head_of_lane(M)
    lane = lax.broadcasted_iota(jnp.int32, (M, E), 1)
    totals = []
    for i in range(CB):
        at = slice(i * rows, (i + 1) * rows)
        p = jnp.exp2(dot_nt(qbd[...], k[at])).astype(BF16)
        o = dot_nt(jnp.concatenate([v[:, at], ones], axis=0), p)
        w = [o[h * HW : (h + 1) * HW, h * M : (h + 1) * M] for h in range(HEADS)]
        totals += [o[E : E + 1, h * M : (h + 1) * M] for h in range(HEADS)]
        part[pl.ds(pl.multiple_of((c0 + i) * M, M), M), :] = jnp.concatenate(w, axis=0).astype(BF16)
    at = pl.ds(pl.multiple_of(cols * M + c0 * HEADS, CB * HEADS), CB * HEADS)
    part[at, :] = jnp.concatenate(totals, axis=0).astype(BF16)


def add_up(gathered, sums):
    sums[...] = sum(gathered[i].astype(F32) for i in range(gathered.shape[0]))


def finish(b, cols, sums, pseudo, proj, up, down, norm, sharp, kbd, vbd, vbt):
    gains = norm[b]
    head_s = lax.broadcasted_iota(jnp.int32, (E, M), 0) // HW
    extra = lax.broadcasted_iota(jnp.int32, (EX - E, M), 0)
    ones = spread_heads(jnp.ones((M, E), F32)).astype(BF16)
    for c0 in range(0, cols, FB):
        blended = []
        for c in range(c0, c0 + FB):
            w = sums[c * M : (c + 1) * M, :].astype(F32)
            row = cols * M + c * HEADS // 16 * 16
            tot = sums[row : row + 16, :].astype(F32)
            f = c * HEADS % 16
            pieces = [w[h * HW : (h + 1) * HW] / tot[f + h : f + h + 1] for h in range(HEADS)]
            blended.append(jnp.transpose(jnp.concatenate(pieces, axis=0)).astype(BF16))
        anchor = jnp.concatenate([pseudo[b].astype(F32)] * FB, axis=0)
        summary = anchor + dot(jnp.concatenate(blended, axis=0), proj[b, 0, 3])
        hidden = gelu(dot(layer_norm(summary, gains[2:3]).astype(BF16), up[b, 0]))
        refined = summary + dot(hidden, down[b, 0])
        n = layer_norm(refined, gains[1:2]).astype(BF16)
        k = scaled_lanes(unit(dot(n, proj[b, 1, 1])), lambda h: sharp[b, 1, h])
        v = dot(n, proj[b, 1, 2])
        for i in range(FB):
            rows = slice(i * M, (i + 1) * M)
            kbd[c0 + i] = spread_heads(k[rows]).astype(BF16)
            if OT == "t":
                vt = jnp.transpose(v[rows])
                for h in range(HEADS):
                    lanes = slice(h * M, (h + 1) * M)
                    vbt[c0 + i, 0:E, lanes] = jnp.where(head_s == h, vt, 0.0).astype(BF16)
                    vbt[c0 + i, E:, lanes] = jnp.where(extra == h, 1.0, 0.0).astype(BF16)
            else:
                vbd[c0 + i, :, 0:E] = spread_heads(v[rows]).astype(BF16)
                vbd[c0 + i, :, E:] = ones


def prepare_row(b, proj, up, down, norm, wout, wup, wdown, avg):
    wout[0:E, 0:E] = proj[b, 1, 3]
    wout[0:E, E:] = dot(proj[b, 1, 3], centering()).astype(BF16)
    wout[E:, 0:E] = identity()
    wout[E:, E:] = centering()
    wup[...] = (as_column(norm[b, 3:4, :]) * up[b, 1].astype(F32)).astype(BF16)
    wdown[:, 0:E] = down[b, 1]
    wdown[:, E:] = dot(down[b, 1], centering()).astype(BF16)
    avg[...] = averaging()


def row_block(c0, x, q, rows, kbd, vbd, vbt, wout, wup, wdown, avg):
    parts = []
    for i in range(CB):
        if OT == "t":
            p = jnp.exp2(dot_nt(kbd[c0 + i], q[i])).astype(BF16)
            o = dot(vbt[c0 + i], p)
            over = 1.0 / o[E : E + 8]
            att = [o[h * HW : (h + 1) * HW] * over[h : h + 1] for h in range(HEADS)]
            att = jnp.transpose(jnp.concatenate(att, axis=0)).astype(BF16)
        else:
            p = jnp.exp2(dot_nt(q[i], kbd[c0 + i])).astype(BF16)
            o = dot(p, vbd[c0 + i])
            att = (o[:, :E] / o[:, E:]).astype(BF16)
        parts.append(jnp.concatenate([att, x[i]], axis=1) if WO == "mxu" else att)
    if WO == "mxu":
        uc = dot(jnp.concatenate(parts, axis=0), wout[...])
        u, c = uc[:, :E], uc[:, E:]
    else:
        u = x[...].reshape(CB * rows, E).astype(F32) + dot(jnp.concatenate(parts, axis=0), wout[0:E, 0:E])
        c = u - jnp.mean(u, axis=-1, keepdims=True)
    hidden = gelu(dot(standardized(c, avg[...]), wup[...]))
    yc = dot(hidden, wdown[...])
    return u + yc[:, :E], c + yc[:, E:]


def first_kernel(cols, t, pseudo, proj, norm, sharp, x_out, q_out, part, xs, qbd, wkvq, wv, avg):
    c0 = pl.program_id(0) * CB
    rows = x_out.shape[1]

    @pl.when(c0 == 0)
    def _():
        prepare_inducing(0, pseudo, proj, norm, sharp, qbd, wkvq, wv, avg)
        part[cols * M :, :] = jnp.zeros((part.shape[0] - cols * M, E), BF16)
        step = 64

        def widen(i, _):
            block = t[pl.ds(i * step, step)].astype(F32)
            xs[pl.ds(i * step * cols, step * cols), :] = block.reshape(step * cols, E)
            return 0

        lax.fori_loop(0, rows // step, widen, 0)

    x = jnp.concatenate([xs[pl.ds(c0 + i, rows, stride=cols), :].astype(BF16) for i in range(CB)], axis=0)
    x_out[...] = x.reshape(CB, rows, E)
    inducing_block(c0, cols, dot(x, centering()), rows, wkvq, wv, qbd, avg, q_out, part)


def mid_kernel(cols, x_in, q_in, gathered, pseudo, proj, up, down, norm, sharp,
               x_out, q_out, part, sums, kbd, vbd, vbt, wout, wup, wdown, qbd, wkvq, wv, avg):
    c0 = pl.program_id(0) * CB
    rows = x_out.shape[1]

    @pl.when(c0 == 0)
    def _():
        prepare_row(0, proj, up, down, norm, wout, wup, wdown, avg)
        prepare_inducing(1, pseudo, proj, norm, sharp, qbd, wkvq, wv, avg)
        part[cols * M :, :] = jnp.zeros((part.shape[0] - cols * M, E), BF16)
        add_up(gathered, sums)
        finish(0, cols, sums, pseudo, proj, up, down, norm, sharp, kbd, vbd, vbt)

    y, c = row_block(c0, x_in, q_in, rows, kbd, vbd, vbt, wout, wup, wdown, avg)
    x_out[...] = y.astype(BF16).reshape(CB, rows, E)
    inducing_block(c0, cols, c, rows, wkvq, wv, qbd, avg, q_out, part)


def last_kernel(cols, x_in, q_in, gathered, pseudo, proj, up, down, norm, sharp,
                y_out, ys, sums, kbd, vbd, vbt, wout, wup, wdown, avg):
    c0 = pl.program_id(0) * CB
    rows = x_in.shape[1]

    @pl.when(c0 == 0)
    def _():
        prepare_row(1, proj, up, down, norm, wout, wup, wdown, avg)
        add_up(gathered, sums)
        finish(1, cols, sums, pseudo, proj, up, down, norm, sharp, kbd, vbd, vbt)

    y, _ = row_block(c0, x_in, q_in, rows, kbd, vbd, vbt, wout, wup, wdown, avg)
    for i in range(CB):
        ys[pl.ds(c0 + i, rows, stride=cols), :] = y[i * rows : (i + 1) * rows]

    @pl.when(c0 == cols - CB)
    def _():
        step = 64

        def narrow(i, _):
            block = ys[pl.ds(i * step * cols, step * cols), :].astype(BF16)
            y_out[pl.ds(i * step, step)] = block.reshape(step, cols, E)
            return 0

        lax.fori_loop(0, rows // step, narrow, 0)


def whole(a):
    return pl.BlockSpec(a.shape, lambda *_: (0,) * a.ndim)


def column(rows):
    return pl.BlockSpec((CB, rows, E), lambda c: (c, 0, 0))


SM = pl.BlockSpec(memory_space=pltpu.SMEM)


def shape(dims, dtype=BF16):
    return jax.ShapeDtypeStruct(dims, dtype)


def ind_scratch():
    return [pltpu.VMEM((HEADS * M, E), BF16), pltpu.VMEM((E, 2 * E), BF16), pltpu.VMEM((E, E), BF16), pltpu.VMEM((E, E), BF16)]


def row_scratch(cols, size):
    return [
        pltpu.VMEM((size, E), F32),
        pltpu.VMEM((cols, HEADS * M, E), BF16),
        pltpu.VMEM((cols, HEADS * M, 2 * E), BF16),
        pltpu.VMEM((cols, EX, HEADS * M), BF16),
        pltpu.VMEM((2 * E, 2 * E), BF16),
        pltpu.VMEM((E, FF), BF16),
        pltpu.VMEM((FF, 2 * E), BF16),
    ]


def first(t, pseudo, proj, norm, sharp, group, cols, size):
    rows, total, _ = t.shape
    return pl.pallas_call(
        functools.partial(first_kernel, cols),
        grid=(cols // CB,),
        in_specs=[pl.BlockSpec((rows, cols, E), lambda c: (0, group, 0)), whole(pseudo), whole(proj), whole(norm), SM],
        out_specs=[column(rows), column(rows), pl.BlockSpec((size, E), lambda c: (0, 0))],
        out_shape=[shape((cols, rows, E)), shape((cols, rows, E)), shape((size, E))],
        scratch_shapes=[pltpu.VMEM((rows * cols, E), F32), *ind_scratch()],
        name="first",
    )(t, pseudo, proj, norm, sharp)


def mid(x, q, sums, pseudo, proj, up, down, norm, sharp, size):
    cols, rows, _ = x.shape
    return pl.pallas_call(
        functools.partial(mid_kernel, cols),
        grid=(cols // CB,),
        in_specs=[column(rows), column(rows), whole(sums), whole(pseudo), whole(proj), whole(up), whole(down), whole(norm), SM],
        out_specs=[column(rows), column(rows), pl.BlockSpec((size, E), lambda c: (0, 0))],
        out_shape=[shape((cols, rows, E)), shape((cols, rows, E)), shape((size, E))],
        scratch_shapes=[*row_scratch(cols, sums.shape[1]), *ind_scratch()],
        name="mid",
    )(x, q, sums, pseudo, proj, up, down, norm, sharp)


def last(x, q, sums, pseudo, proj, up, down, norm, sharp):
    cols, rows, _ = x.shape
    return pl.pallas_call(
        functools.partial(last_kernel, cols),
        grid=(cols // CB,),
        in_specs=[column(rows), column(rows), whole(sums), whole(pseudo), whole(proj), whole(up), whole(down), whole(norm), SM],
        out_specs=pl.BlockSpec((rows, cols, E), lambda c: (0, 0, 0)),
        out_shape=shape((rows, cols, E)),
        scratch_shapes=[pltpu.VMEM((rows * cols, E), F32), *row_scratch(cols, sums.shape[1]), pltpu.VMEM((E, E), BF16)],
        name="last",
    )(x, q, sums, pseudo, proj, up, down, norm, sharp)


def gathered_parts(part):
    return lax.all_gather(part, "row")


def body(t, pseudo, proj, up, down, norm, sharp):
    feat, ways = lax.axis_size("feat"), lax.axis_size("row")
    rows, total, _ = t.shape
    groups = 2
    cols = total // groups
    size = cols * (M + HEADS)
    padded = -(-size // (8 * ways)) * 8 * ways
    weights = (pseudo, proj, up, down, norm, sharp)
    xa, qa, pa = first(t, pseudo, proj, norm, sharp, 0, cols, size)
    sa = gathered_parts(pa)
    t, pa = lax.optimization_barrier((t, pa))
    xb, qb, pb = first(t, pseudo, proj, norm, sharp, 1, cols, padded)
    pieces = lax.all_to_all(pb.reshape(ways, padded // ways, E), "row", 0, 0, tiled=True)
    piece = jnp.sum(pieces.astype(F32), axis=0).astype(BF16)
    piece, xa = lax.optimization_barrier((piece, xa))
    sb = lax.all_to_all(jnp.broadcast_to(piece, pieces.shape), "row", 0, 0, tiled=True)
    xa, qa, pa = mid(xa, qa, sa, *weights, size)
    sa = gathered_parts(pa)
    xb, pa = lax.optimization_barrier((xb, pa))
    xb, qb, pb = mid(xb, qb, sb.reshape(1, padded, E), *weights, size)
    sb = gathered_parts(pb)
    y = [last(xa, qa, sa, *weights), last(xb, qb, sb, *weights)]
    y = [lax.all_to_all(v.reshape(feat, rows // feat, cols, E), "feat", 0, 0, tiled=True) for v in y]
    y = jnp.stack(y, axis=2)
    return jnp.transpose(y, (1, 0, 2, 3, 4)).reshape(rows // feat, feat * total, E)


def solution(mesh):
    return jax.shard_map(
        body,
        mesh=mesh,
        in_specs=(P("row", "feat", None), P(), P(), P(), P(), P(), P()),
        out_specs=P(("row", "feat"), None, None),
        check_vma=False,
    )
```

```python
import functools
import jax
import jax.numpy as jnp
from jax import lax
from jax.experimental import pallas as pl
from jax.experimental.pallas import tpu as pltpu
from jax.sharding import PartitionSpec as P

F32, BF16 = jnp.float32, jnp.bfloat16
LOG2E = 1.4426950408889634
HEADS, HW, E, M, FF = 4, 32, 128, 128, 256
NT = (((1,), (1,)), ((), ()))
CB = 2
PV = "t"
WO = "mxu"
OT = "t"
EX = E + 16
FB = 8
UNIT = "xlu"
VAR = "xlu"
GELU = "f32"


def dot(a, b):
    return jnp.dot(a, b, preferred_element_type=F32)


def dot_nt(a, b):
    return lax.dot_general(a, b, NT, preferred_element_type=F32)


def layer_norm(x, gain):
    c = x - jnp.mean(x, axis=-1, keepdims=True)
    v = jnp.mean(c * c, axis=-1, keepdims=True)
    return c * lax.rsqrt(v + 1e-5) * gain


def unit(x):
    return x * lax.rsqrt(jnp.mean(x * x, axis=-1, keepdims=True) + 1e-6)


def gelu(x):
    if GELU == "bf16":
        x = x.astype(BF16)
        inner = x * (BF16(0.7978845608028654) + BF16(0.7978845608028654 * 0.044715) * (x * x))
        half = BF16(0.5) * x
        return half + half * jnp.tanh(inner)
    inner = x * (0.7978845608028654 + (0.7978845608028654 * 0.044715) * (x * x))
    half = 0.5 * x
    return (half + half * jnp.tanh(inner)).astype(BF16)


def head_of_lane(rows):
    return lax.broadcasted_iota(jnp.int32, (rows, E), 1) // HW


def averaging():
    return jnp.full((E, E), 1.0 / E, BF16)


def centering():
    eye = lax.broadcasted_iota(jnp.int32, (E, E), 0) == lax.broadcasted_iota(jnp.int32, (E, E), 1)
    return jnp.where(eye, 1.0 - 1.0 / E, -1.0 / E).astype(BF16)


def identity():
    eye = lax.broadcasted_iota(jnp.int32, (E, E), 0) == lax.broadcasted_iota(jnp.int32, (E, E), 1)
    return jnp.where(eye, 1.0, 0.0).astype(BF16)


def as_column(row):
    eye = lax.broadcasted_iota(jnp.int32, (E, E), 0) == lax.broadcasted_iota(jnp.int32, (E, E), 1)
    return jnp.sum(jnp.where(eye, row, 0.0), axis=1, keepdims=True)


def standardized(c, average):
    if VAR == "mxu":
        v = dot((c * c).astype(BF16), average)
    else:
        v = jnp.mean(c * c, axis=-1, keepdims=True)
    return (c * lax.rsqrt(v + 1e-5)).astype(BF16)


def scaled_lanes(values, sharp_row):
    head = head_of_lane(1)
    scale = jnp.zeros((1, E), F32)
    for h in range(HEADS):
        scale = jnp.where(head == h, sharp_row(h) * (LOG2E / HW), scale)
    return values * scale


def spread_heads(values):
    head = head_of_lane(values.shape[0])
    zero = jnp.zeros_like(values)
    return jnp.concatenate([jnp.where(head == h, values, zero) for h in range(HEADS)], axis=0)


def prepare_inducing(b, pseudo, proj, norm, sharp, qbd, wkvq, wv, avg):
    q = unit(dot(pseudo[b], proj[b, 0, 0]))
    q = scaled_lanes(q, lambda h: sharp[b, 0, h])
    qbd[...] = spread_heads(q).astype(BF16)
    gain = as_column(norm[b, 0:1, :])
    wkvq[:, 0:E] = (gain * proj[b, 0, 1].astype(F32)).astype(BF16)
    wkvq[:, E : 2 * E] = (gain * proj[b, 1, 0].astype(F32)).astype(BF16)
    wv[...] = (jnp.transpose(proj[b, 0, 2].astype(F32)) * norm[b, 0:1, :]).astype(BF16)
    avg[...] = averaging()


def inducing_block(c0, cols, c, rows, wkvq, wv, qbd, avg, q_out, part):
    count = c.shape[0] // rows
    n = standardized(c, avg[...])
    if PV == "t":
        kq = dot(n, wkvq[:, : 2 * E])
        k, q = unit(kq[:, :E]).astype(BF16), unit(kq[:, E:]).astype(BF16)
        v = dot_nt(wv[...], n).astype(BF16)
        ones = jnp.ones((EX - E, rows), BF16)
    else:
        kvq = dot(n, wkvq[...])
        k, q = unit(kvq[:, :E]).astype(BF16), unit(kvq[:, E : 2 * E]).astype(BF16)
        v = kvq[:, 2 * E :].astype(BF16)
        ones = jnp.ones((rows, E), BF16)
    q_out[...] = q.reshape(q_out.shape)
    head = head_of_lane(M)
    lane = lax.broadcasted_iota(jnp.int32, (M, E), 1)
    totals = []
    for i in range(count):
        at = slice(i * rows, (i + 1) * rows)
        p = jnp.exp2(dot_nt(qbd[...], k[at])).astype(BF16)
        o = dot_nt(jnp.concatenate([v[:, at], ones], axis=0), p)
        w = [o[h * HW : (h + 1) * HW, h * M : (h + 1) * M] for h in range(HEADS)]
        totals += [o[E : E + 1, h * M : (h + 1) * M] for h in range(HEADS)]
        part[pl.ds(pl.multiple_of((c0 + i) * M, M), M), :] = jnp.concatenate(w, axis=0).astype(BF16)
    at = pl.ds(pl.multiple_of(cols * M + c0 * HEADS, count * HEADS), count * HEADS)
    part[at, :] = jnp.concatenate(totals, axis=0).astype(BF16)


def add_up(gathered, sums):
    sums[...] = sum(gathered[i].astype(F32) for i in range(gathered.shape[0]))


def finish(b, cols, sums, pseudo, proj, up, down, norm, sharp, kbd, vbd, vbt):
    gains = norm[b]
    head_s = lax.broadcasted_iota(jnp.int32, (E, M), 0) // HW
    extra = lax.broadcasted_iota(jnp.int32, (EX - E, M), 0)
    ones = spread_heads(jnp.ones((M, E), F32)).astype(BF16)
    for c0 in range(0, cols, FB):
        blended = []
        for c in range(c0, c0 + FB):
            w = sums[c * M : (c + 1) * M, :].astype(F32)
            row = cols * M + c * HEADS // 16 * 16
            tot = sums[row : row + 16, :].astype(F32)
            f = c * HEADS % 16
            pieces = [w[h * HW : (h + 1) * HW] / tot[f + h : f + h + 1] for h in range(HEADS)]
            blended.append(jnp.transpose(jnp.concatenate(pieces, axis=0)).astype(BF16))
        anchor = jnp.concatenate([pseudo[b].astype(F32)] * FB, axis=0)
        summary = anchor + dot(jnp.concatenate(blended, axis=0), proj[b, 0, 3])
        hidden = gelu(dot(layer_norm(summary, gains[2:3]).astype(BF16), up[b, 0]))
        refined = summary + dot(hidden, down[b, 0])
        n = layer_norm(refined, gains[1:2]).astype(BF16)
        k = scaled_lanes(unit(dot(n, proj[b, 1, 1])), lambda h: sharp[b, 1, h])
        v = dot(n, proj[b, 1, 2])
        for i in range(FB):
            rows = slice(i * M, (i + 1) * M)
            kbd[c0 + i] = spread_heads(k[rows]).astype(BF16)
            if OT == "t":
                vt = jnp.transpose(v[rows])
                for h in range(HEADS):
                    lanes = slice(h * M, (h + 1) * M)
                    vbt[c0 + i, 0:E, lanes] = jnp.where(head_s == h, vt, 0.0).astype(BF16)
                    vbt[c0 + i, E:, lanes] = jnp.where(extra == h, 1.0, 0.0).astype(BF16)
            else:
                vbd[c0 + i, :, 0:E] = spread_heads(v[rows]).astype(BF16)
                vbd[c0 + i, :, E:] = ones


def prepare_row(b, proj, up, down, norm, wout, wup, wdown, avg):
    wout[0:E, 0:E] = proj[b, 1, 3]
    wout[0:E, E:] = dot(proj[b, 1, 3], centering()).astype(BF16)
    wout[E:, 0:E] = identity()
    wout[E:, E:] = centering()
    wup[...] = (as_column(norm[b, 3:4, :]) * up[b, 1].astype(F32)).astype(BF16)
    wdown[:, 0:E] = down[b, 1]
    wdown[:, E:] = dot(down[b, 1], centering()).astype(BF16)
    avg[...] = averaging()


def row_block(c0, x, q, rows, kbd, vbd, vbt, wout, wup, wdown, avg):
    parts = []
    for i in range(CB):
        if OT == "t":
            p = jnp.exp2(dot_nt(kbd[c0 + i], q[i])).astype(BF16)
            o = dot(vbt[c0 + i], p)
            over = 1.0 / o[E : E + 8]
            att = [o[h * HW : (h + 1) * HW] * over[h : h + 1] for h in range(HEADS)]
            att = jnp.transpose(jnp.concatenate(att, axis=0)).astype(BF16)
        else:
            p = jnp.exp2(dot_nt(q[i], kbd[c0 + i])).astype(BF16)
            o = dot(p, vbd[c0 + i])
            att = (o[:, :E] / o[:, E:]).astype(BF16)
        parts.append(jnp.concatenate([att, x[i]], axis=1) if WO == "mxu" else att)
    if WO == "mxu":
        uc = dot(jnp.concatenate(parts, axis=0), wout[...])
        u, c = uc[:, :E], uc[:, E:]
    else:
        u = x[...].reshape(CB * rows, E).astype(F32) + dot(jnp.concatenate(parts, axis=0), wout[0:E, 0:E])
        c = u - jnp.mean(u, axis=-1, keepdims=True)
    hidden = gelu(dot(standardized(c, avg[...]), wup[...]))
    yc = dot(hidden, wdown[...])
    return u + yc[:, :E], c + yc[:, E:]


def first_kernel(cols, t, pseudo, proj, norm, sharp, x_out, q_out, part, xs, qbd, wkvq, wv, avg):
    count = x_out.shape[0]
    c0 = pl.program_id(0) * count
    rows = x_out.shape[1]

    @pl.when(c0 == 0)
    def _():
        prepare_inducing(0, pseudo, proj, norm, sharp, qbd, wkvq, wv, avg)
        part[cols * M :, :] = jnp.zeros((part.shape[0] - cols * M, E), BF16)
        step = 64

        def widen(i, _):
            block = t[pl.ds(i * step, step)].astype(F32)
            xs[pl.ds(i * step * cols, step * cols), :] = block.reshape(step * cols, E)
            return 0

        lax.fori_loop(0, rows // step, widen, 0)

    x = jnp.concatenate([xs[pl.ds(c0 + i, rows, stride=cols), :].astype(BF16) for i in range(count)], axis=0)
    x_out[...] = x.reshape(count, rows, E)
    inducing_block(c0, cols, dot(x, centering()), rows, wkvq, wv, qbd, avg, q_out, part)


def mid_kernel(cols, x_in, q_in, gathered, pseudo, proj, up, down, norm, sharp,
               x_out, q_out, part, sums, kbd, vbd, vbt, wout, wup, wdown, qbd, wkvq, wv, avg):
    c0 = pl.program_id(0) * CB
    rows = x_out.shape[1]

    @pl.when(c0 == 0)
    def _():
        prepare_row(0, proj, up, down, norm, wout, wup, wdown, avg)
        prepare_inducing(1, pseudo, proj, norm, sharp, qbd, wkvq, wv, avg)
        part[cols * M :, :] = jnp.zeros((part.shape[0] - cols * M, E), BF16)
        add_up(gathered, sums)
        finish(0, cols, sums, pseudo, proj, up, down, norm, sharp, kbd, vbd, vbt)

    y, c = row_block(c0, x_in, q_in, rows, kbd, vbd, vbt, wout, wup, wdown, avg)
    x_out[...] = y.astype(BF16).reshape(CB, rows, E)
    inducing_block(c0, cols, c, rows, wkvq, wv, qbd, avg, q_out, part)


def last_kernel(cols, x_in, q_in, gathered, pseudo, proj, up, down, norm, sharp,
                y_out, ys, sums, kbd, vbd, vbt, wout, wup, wdown, avg):
    c0 = pl.program_id(0) * CB
    rows = x_in.shape[1]

    @pl.when(c0 == 0)
    def _():
        prepare_row(1, proj, up, down, norm, wout, wup, wdown, avg)
        add_up(gathered, sums)
        finish(1, cols, sums, pseudo, proj, up, down, norm, sharp, kbd, vbd, vbt)

    y, _ = row_block(c0, x_in, q_in, rows, kbd, vbd, vbt, wout, wup, wdown, avg)
    for i in range(CB):
        ys[pl.ds(c0 + i, rows, stride=cols), :] = y[i * rows : (i + 1) * rows]

    @pl.when(c0 == cols - CB)
    def _():
        step = 64

        def narrow(i, _):
            block = ys[pl.ds(i * step * cols, step * cols), :].astype(BF16)
            y_out[pl.ds(i * step, step)] = block.reshape(step, cols, E)
            return 0

        lax.fori_loop(0, rows // step, narrow, 0)


def whole(a):
    return pl.BlockSpec(a.shape, lambda *_: (0,) * a.ndim)


def column(rows, count=CB):
    return pl.BlockSpec((count, rows, E), lambda c: (c, 0, 0))


SM = pl.BlockSpec(memory_space=pltpu.SMEM)


def shape(dims, dtype=BF16):
    return jax.ShapeDtypeStruct(dims, dtype)


def ind_scratch():
    return [pltpu.VMEM((HEADS * M, E), BF16), pltpu.VMEM((E, 2 * E), BF16), pltpu.VMEM((E, E), BF16), pltpu.VMEM((E, E), BF16)]


def row_scratch(cols, size):
    return [
        pltpu.VMEM((size, E), F32),
        pltpu.VMEM((cols, HEADS * M, E), BF16),
        pltpu.VMEM((cols, HEADS * M, 2 * E), BF16),
        pltpu.VMEM((cols, EX, HEADS * M), BF16),
        pltpu.VMEM((2 * E, 2 * E), BF16),
        pltpu.VMEM((E, FF), BF16),
        pltpu.VMEM((FF, 2 * E), BF16),
    ]


def first(t, pseudo, proj, norm, sharp, group, cols, size):
    rows, total, _ = t.shape
    return pl.pallas_call(
        functools.partial(first_kernel, cols),
        grid=(cols // 4,),
        in_specs=[pl.BlockSpec((rows, cols, E), lambda c: (0, group, 0)), whole(pseudo), whole(proj), whole(norm), SM],
        out_specs=[column(rows, 4), column(rows, 4), pl.BlockSpec((size, E), lambda c: (0, 0))],
        out_shape=[shape((cols, rows, E)), shape((cols, rows, E)), shape((size, E))],
        scratch_shapes=[pltpu.VMEM((rows * cols, E), F32), *ind_scratch()],
        name="first",
    )(t, pseudo, proj, norm, sharp)


def mid(x, q, sums, pseudo, proj, up, down, norm, sharp, size):
    cols, rows, _ = x.shape
    return pl.pallas_call(
        functools.partial(mid_kernel, cols),
        grid=(cols // CB,),
        in_specs=[column(rows), column(rows), whole(sums), whole(pseudo), whole(proj), whole(up), whole(down), whole(norm), SM],
        out_specs=[column(rows), column(rows), pl.BlockSpec((size, E), lambda c: (0, 0))],
        out_shape=[shape((cols, rows, E)), shape((cols, rows, E)), shape((size, E))],
        scratch_shapes=[*row_scratch(cols, sums.shape[1]), *ind_scratch()],
        name="mid",
    )(x, q, sums, pseudo, proj, up, down, norm, sharp)


def last(x, q, sums, pseudo, proj, up, down, norm, sharp):
    cols, rows, _ = x.shape
    return pl.pallas_call(
        functools.partial(last_kernel, cols),
        grid=(cols // CB,),
        in_specs=[column(rows), column(rows), whole(sums), whole(pseudo), whole(proj), whole(up), whole(down), whole(norm), SM],
        out_specs=pl.BlockSpec((rows, cols, E), lambda c: (0, 0, 0)),
        out_shape=shape((rows, cols, E)),
        scratch_shapes=[pltpu.VMEM((rows * cols, E), F32), *row_scratch(cols, sums.shape[1]), pltpu.VMEM((E, E), BF16)],
        name="last",
    )(x, q, sums, pseudo, proj, up, down, norm, sharp)


def gathered_parts(part):
    return lax.all_gather(part, "row")


def body(t, pseudo, proj, up, down, norm, sharp):
    feat, ways = lax.axis_size("feat"), lax.axis_size("row")
    rows, total, _ = t.shape
    groups = 2
    cols = total // groups
    size = cols * (M + HEADS)
    padded = -(-size // (8 * ways)) * 8 * ways
    weights = (pseudo, proj, up, down, norm, sharp)
    xa, qa, pa = first(t, pseudo, proj, norm, sharp, 0, cols, size)
    sa = gathered_parts(pa)
    t, pa = lax.optimization_barrier((t, pa))
    xb, qb, pb = first(t, pseudo, proj, norm, sharp, 1, cols, padded)
    pieces = lax.all_to_all(pb.reshape(ways, padded // ways, E), "row", 0, 0, tiled=True)
    piece = jnp.sum(pieces.astype(F32), axis=0).astype(BF16)
    piece, xa = lax.optimization_barrier((piece, xa))
    sb = lax.all_to_all(jnp.broadcast_to(piece, pieces.shape), "row", 0, 0, tiled=True)
    xa, qa, pa = mid(xa, qa, sa, *weights, size)
    sa = gathered_parts(pa)
    xb, pa = lax.optimization_barrier((xb, pa))
    xb, qb, pb = mid(xb, qb, sb.reshape(1, padded, E), *weights, size)
    sb = gathered_parts(pb)
    y = [last(xa, qa, sa, *weights), last(xb, qb, sb, *weights)]
    y = [lax.all_to_all(v.reshape(feat, rows // feat, cols, E), "feat", 0, 0, tiled=True) for v in y]
    y = jnp.stack(y, axis=2)
    return jnp.transpose(y, (1, 0, 2, 3, 4)).reshape(rows // feat, feat * total, E)


def solution(mesh):
    return jax.shard_map(
        body,
        mesh=mesh,
        in_specs=(P("row", "feat", None), P(), P(), P(), P(), P(), P()),
        out_specs=P(("row", "feat"), None, None),
        check_vma=False,
    )
```
